256 devices in a mesh: pb: 16 (over z, x_hi), kv: 16 (over x_lo, y, core).
Axes of the slice: x: 4 (x_hi: 2, x_lo: 2; x = x_hi * 2 + x_lo), y: 4, z: 8, core: 2. Of those that a mesh axis runs over, the one named last changes fastest.
Arguments:
- queries: bfloat16 [32768, 1024], P(('pb', 'kv')), may hold values from -6 to 6
- key_rows: bfloat16 [32768, 128], P(('pb', 'kv')), may hold values from -6 to 6
- value_rows: bfloat16 [32768, 128], P(('pb', 'kv')), may hold values from -6 to 6
- out_grad: bfloat16 [32768, 1024], P(('pb', 'kv')), may hold values from -6 to 6
- doc_ids: int32 [256], replicated, may hold values from 0 to 63, never falling along the last dimension, each value on 1 to 16 neighbouring positions
Outputs:
- attended: bfloat16 [32768, 1024], P(('pb', 'kv'))
- query_grad: bfloat16 [32768, 1024], P(('pb', 'kv'))
- key_grad: bfloat16 [32768, 128], P(('pb', 'kv'))
- value_grad: bfloat16 [32768, 128], P(('pb', 'kv'))
The draws below stay inside these ranges and needn't reach their ends.
Inputs may be any that keep to these rules, and one draw needn't show every extreme that they name: `doc_ids`: ids never fall along the sequence; each document covers 1 to 16 consecutive blocks, and one covers exactly 16.
All inputs are finite; a program needn't handle non-finite values.
Results may differ from the reference program's by a relative error of at most 0.03.
Values may be sent and summed in bfloat16 or wider, within the bound.
A program may use at most 64 MiB of HBM per device.

```python
import math
import jax
import jax.numpy as jnp
import numpy as np
from jax import lax

HEADS = 8
HEAD_DIM = 128
BLOCK = 128
LEN = 32768
NBLK = 256
MOST = 16
DOCS = 64


def draw_queries(key, part):
    sample_key = jax.random.fold_in(key, 1)
    sample = jax.random.truncated_normal(sample_key, -6.0, 6.0, (NBLK, BLOCK, HEADS, HEAD_DIM), jnp.float32)
    return sample.reshape(LEN, HEADS * HEAD_DIM).astype(jnp.bfloat16)


def draw_key_rows(key, part):
    sample_key = jax.random.fold_in(key, 2)
    sample = jax.random.truncated_normal(sample_key, -6.0, 6.0, (NBLK, BLOCK, HEAD_DIM), jnp.float32)
    return sample.reshape(LEN, HEAD_DIM).astype(jnp.bfloat16)


def block_levels(key, dims, shards, smallest, high):
    factor_of, own = 1.0, jax.random.fold_in(key, 6)
    for axis_at, shards_of in shards:
        heights = jnp.exp(jax.random.uniform(jax.random.fold_in(own, axis_at), (shards_of,), jnp.float32, smallest / len(shards), high / len(shards)))
        factor_of = factor_of * jnp.repeat(heights, dims[axis_at] // shards_of).reshape([-1 if axis == axis_at else 1 for axis in range(len(dims))])
    return factor_of


def profile(count, total, bound, skew):
    portions = [(1 << 20) // math.isqrt(rank ** skew) + 1 for rank in range(2, count + 1)]
    spare, counts = total - bound - (count - 1), [1] * (count - 1)
    while spare > 0:
        candidates = [i for i in range(count - 1) if counts[i] < bound]
        mass, left = sum([portions[i] for i in candidates]), spare
        for i in candidates:
            more = min(bound - counts[i], max(1, left * portions[i] // mass), spare)
            counts[i] = counts[i] + more
            spare = spare - more
    return np.array([bound] + counts)


def uneven_parts(rng, number_of, total, reach, slope):
    if number_of == 2:
        one = jax.random.randint(rng, (), max(1, total - reach), min(reach, total - 1) + 1)
        return jnp.stack([one, total - one])
    sizes = jnp.asarray(profile(number_of, total, reach, slope), jnp.int32)
    pairs = (number_of - 1) // 2
    giver, receiver = sizes[1:1 + 2 * pairs:2], sizes[2:2 + 2 * pairs:2]
    room = jnp.minimum(giver - 1, reach - receiver)
    shifted = jax.random.randint(jax.random.fold_in(rng, 1), (pairs,), 0, 1 << 20) % (room + 1)
    sizes = sizes.at[1:1 + 2 * pairs:2].set(giver - shifted).at[2:2 + 2 * pairs:2].set(receiver + shifted)
    return sizes[jax.random.permutation(jax.random.fold_in(rng, 2), number_of)]


def centred(key, shape, spread, bound, cuts=(), kind=jnp.bfloat16):
    level = block_levels(key, shape, cuts, -0.22, 0.18) if cuts else 1.0
    drawn = jax.random.normal(key, shape, jnp.float32) * spread * level
    return jnp.minimum(jnp.maximum(drawn, -bound), bound).astype(kind)


def setup_inputs(seed: int = 0) -> dict:
    streams_of = jax.random.split(jax.random.key(seed), 6)
    queries = draw_queries(jax.random.fold_in(streams_of[5], 71), 0)
    key_rows = draw_key_rows(jax.random.fold_in(streams_of[5], 71), 0)
    value_rows = centred(streams_of[2], (LEN, HEAD_DIM), 1.0, 6.0, ((0, 256),))
    out_grad = centred(streams_of[3], (LEN, HEADS * HEAD_DIM), 1.0, 6.0, ((0, 256),))
    doc_ids = jnp.searchsorted(jnp.cumsum(uneven_parts(streams_of[4], DOCS, NBLK, MOST, 1)), jnp.arange(NBLK), side="right").astype(jnp.int32)
    return dict(queries=queries, key_rows=key_rows, value_rows=value_rows, out_grad=out_grad, doc_ids=doc_ids)


NEG_FILL = -1e30


def reference(queries, key_rows, value_rows, out_grad, doc_ids):
    score_scale = HEAD_DIM ** -0.5
    window_len = MOST * BLOCK
    pad_keys = jnp.concatenate([jnp.zeros((window_len, HEAD_DIM), key_rows.dtype), key_rows], axis=0)
    pad_values = jnp.concatenate([jnp.zeros((window_len, HEAD_DIM), value_rows.dtype), value_rows], axis=0)
    pad_docs = jnp.concatenate([jnp.full((MOST,), -1, jnp.int32), doc_ids.astype(jnp.int32)])
    local_pos = jnp.arange(BLOCK, dtype=jnp.int32)
    window_pos = jnp.arange(window_len, dtype=jnp.int32)

    def window(block_idx):
        win_start = ((block_idx + 1) * BLOCK).astype(jnp.int32)
        keys_win = lax.dynamic_slice_in_dim(pad_keys, win_start, window_len, 0)
        values_win = lax.dynamic_slice_in_dim(pad_values, win_start, window_len, 0)
        docs_win = jnp.repeat(lax.dynamic_slice_in_dim(pad_docs, (block_idx + 1).astype(jnp.int32), MOST, 0), BLOCK)
        query_doc = lax.dynamic_index_in_dim(doc_ids.astype(jnp.int32), block_idx, 0, keepdims=False)
        query_pos = block_idx * BLOCK + local_pos
        key_pos = block_idx * BLOCK + BLOCK - window_len + window_pos
        allowed = (docs_win == query_doc)[None, :] & (key_pos[None, :] <= query_pos[:, None])
        allowed = jnp.repeat(allowed, HEADS, axis=0)
        query_blk = lax.dynamic_slice_in_dim(queries, (block_idx * BLOCK).astype(jnp.int32), BLOCK, 0)
        query_blk = query_blk.reshape(BLOCK * HEADS, HEAD_DIM)
        scores = lax.dot_general(query_blk, keys_win, (((1,), (1,)), ((), ())), preferred_element_type=jnp.float32) * score_scale
        scores = jnp.where(allowed, scores, NEG_FILL)
        return keys_win, values_win, allowed, query_blk, scores

    def forward(block_idx):
        keys_win, values_win, allowed, query_blk, scores = window(block_idx)
        row_max = jnp.max(scores, axis=1)
        row_sum = jnp.sum(jnp.where(allowed, jnp.exp(scores - row_max[:, None]), 0.0), axis=1)
        log_total = row_max + jnp.log(row_sum)
        weights = jnp.where(allowed, jnp.exp(scores - log_total[:, None]), 0.0)
        mixed_rows = jnp.dot(weights.astype(jnp.bfloat16), values_win, preferred_element_type=jnp.float32)
        return mixed_rows.reshape(BLOCK, HEADS * HEAD_DIM).astype(jnp.bfloat16), log_total

    block_list = jnp.arange(NBLK, dtype=jnp.int32)
    attended_blocks, log_totals = lax.map(forward, block_list)
    attended = attended_blocks.reshape(LEN, HEADS * HEAD_DIM)
    delta_all = jnp.sum(out_grad.astype(jnp.float32).reshape(NBLK, BLOCK * HEADS, HEAD_DIM)
                        * attended.astype(jnp.float32).reshape(NBLK, BLOCK * HEADS, HEAD_DIM), axis=2)

    def backward(running, inputs):
        key_acc, value_acc = running
        block_idx, log_total, delta_rows = inputs
        keys_win, values_win, allowed, query_blk, scores = window(block_idx)
        weights = jnp.where(allowed, jnp.exp(scores - log_total[:, None]), 0.0)
        weights_b = weights.astype(jnp.bfloat16)
        grad_blk = lax.dynamic_slice_in_dim(out_grad, (block_idx * BLOCK).astype(jnp.int32), BLOCK, 0)
        grad_blk = grad_blk.reshape(BLOCK * HEADS, HEAD_DIM)
        grad_probs = lax.dot_general(grad_blk, values_win, (((1,), (1,)), ((), ())), preferred_element_type=jnp.float32)
        score_grad = (score_scale * weights * (grad_probs - delta_rows[:, None])).astype(jnp.bfloat16)
        query_part = jnp.dot(score_grad, keys_win, preferred_element_type=jnp.float32)
        key_part = lax.dot_general(score_grad, query_blk, (((0,), (0,)), ((), ())), preferred_element_type=jnp.float32)
        value_part = lax.dot_general(weights_b, grad_blk, (((0,), (0,)), ((), ())), preferred_element_type=jnp.float32)
        win_start = ((block_idx + 1) * BLOCK).astype(jnp.int32)
        key_acc = lax.dynamic_update_slice_in_dim(
            key_acc, lax.dynamic_slice_in_dim(key_acc, win_start, window_len, 0) + key_part, win_start, 0)
        value_acc = lax.dynamic_update_slice_in_dim(
            value_acc, lax.dynamic_slice_in_dim(value_acc, win_start, window_len, 0) + value_part, win_start, 0)
        return (key_acc, value_acc), query_part.reshape(BLOCK, HEADS * HEAD_DIM).astype(jnp.bfloat16)

    start_acc = jnp.zeros((window_len + LEN, HEAD_DIM), jnp.float32)
    final_acc, query_grads = lax.scan(backward, (start_acc, start_acc), (block_list, log_totals, delta_all))
    key_acc, value_acc = final_acc
    query_grad = query_grads.reshape(LEN, HEADS * HEAD_DIM)
    return attended, query_grad, key_acc[window_len:].astype(jnp.bfloat16), value_acc[window_len:].astype(jnp.bfloat16)
```

```python
import jax
import jax.numpy as jnp
from jax import lax
from jax.experimental import pallas as pl
from jax.experimental.pallas import tpu as pltpu
from jax.sharding import PartitionSpec as P

HEADS = 8
HEAD_DIM = 128
BLOCK = 128
NBLK = 256
WIDE = HEADS * HEAD_DIM

NEG = -1e30
SCALE = HEAD_DIM ** (-0.5)
LOG2E = 1.4426950408889634
EXP_SCALE = SCALE * LOG2E

MESH = pl.DeviceIdType.MESH


def dot_nn(a, b):
    return lax.dot_general(a, b, (((1,), (0,)), ((), ())), preferred_element_type=jnp.float32)


def dot_nt(a, b):
    return lax.dot_general(a, b, (((1,), (1,)), ((), ())), preferred_element_type=jnp.float32)


def head_cols(h):
    return slice(h * HEAD_DIM, (h + 1) * HEAD_DIM)


def kernel(
    q_hbm, k_hbm, v_hbm, g_hbm, docs_hbm,
    att_hbm, dq_hbm, dk_hbm, dv_hbm,
    kv, q_in, g_in, qt, gt, probs, maxes, run_max, run_sum, out_acc, dq_acc, delta,
    w_scr, ds_scr, pg, r1r, r2s, r2r, r3s, r3r, att_out, dq_out, dkv_out, docs,
    local_sem, docs_sem,
    x_send, x_recv, y_send, p_send, p_recv,
    r1_send, r1_recv, r2_send, r2_recv, r3_send, r3_recv,
):
    pb = lax.axis_index("pb")
    kvi = lax.axis_index("kv")
    p = pb * 16 + kvi
    c = lax.rem(kvi, 2)
    y = lax.rem(lax.div(kvi, 2), 4)
    col_base = lax.div(kvi, 8) * 8

    def seq_dev(delta_p):
        t = lax.rem(p + delta_p + NBLK, NBLK)
        return (lax.div(t, 16), lax.rem(t, 16))

    def y_dev(k):
        return (pb, col_base + lax.rem(y + k, 4) * 2 + c)

    partner = (pb, kvi + 1 - 2 * c)
    wraps = [None] + [lax.div(y + k, 4) for k in (1, 2, 3)]

    barrier = pltpu.get_barrier_semaphore()
    peers = [seq_dev(8), seq_dev(16), seq_dev(-8), seq_dev(-16), y_dev(1), y_dev(2), y_dev(3), partner]
    for peer in peers:
        pl.semaphore_signal(barrier, inc=1, device_id=peer, device_id_type=MESH)

    own_k = pltpu.make_async_copy(k_hbm, kv.at[0, c, 0], local_sem.at[0])
    own_v = pltpu.make_async_copy(v_hbm, kv.at[0, c, 1], local_sem.at[1])
    own_k.start()
    own_v.start()
    docs_copy = pltpu.make_async_copy(docs_hbm, docs, docs_sem)
    docs_copy.start()
    q_copy = pltpu.make_async_copy(q_hbm, q_in, local_sem.at[2])
    g_copy = pltpu.make_async_copy(g_hbm, g_in, local_sem.at[3])
    q_copy.start()
    g_copy.start()
    own_k.wait()
    own_v.wait()
    pl.semaphore_wait(barrier, len(peers))

    def remote(src, dst, send_sem, recv_sem, dev):
        return pltpu.make_async_remote_copy(
            src_ref=src, dst_ref=dst, send_sem=send_sem, recv_sem=recv_sem,
            device_id=dev, device_id_type=MESH)

    def x_copy(i):
        return remote(kv.at[0, c], kv.at[4 * i, c], x_send.at[i], x_recv.at[4 * i], seq_dev(8 * i))

    def y_copy(k, second):
        wrap = wraps[k]
        e = k + 4 * second
        return remote(kv.at[4 * wrap + 4 * second, c], kv.at[e, c], y_send.at[e], x_recv.at[e], y_dev(k))

    def p_copy(e):
        return remote(kv.at[e, c], kv.at[e, c], p_send.at[e], p_recv.at[e], partner)

    def special_copy():
        return remote(kv.at[8 * c, c], kv.at[0, c], p_send.at[0], p_recv.at[0], partner)

    x_copy(1).start()
    for k in (1, 2, 3):
        @pl.when(wraps[k] == 0)
        def _():
            y_copy(k, 0).start()
    x_copy(2).start()

    q_copy.wait()
    for h in range(HEADS):
        qt[:, head_cols(h)] = q_in[:, head_cols(h)].T
    docs_copy.wait()
    my_doc = docs[p]

    def bias_of(idx):
        same = (docs[jnp.maximum(idx, 0)] == my_doc) & (idx >= 0)
        return jnp.where(same, 0.0, NEG).astype(jnp.float32)

    def forward(keys, values_t, slot, parts, first):
        for h in range(HEADS):
            cols = head_cols(h)
            s = dot_nn(keys, qt[:, cols])
            if first:
                key_at = lax.broadcasted_iota(jnp.int32, s.shape, 0)
                query_at = lax.broadcasted_iota(jnp.int32, s.shape, 1)
                s = jnp.where(key_at <= query_at, s, NEG)
            tops = []
            for lo, _, _, bias in parts:
                top = jnp.max(s[lo:lo + BLOCK], axis=0, keepdims=True) * EXP_SCALE
                tops.append(top if bias is None else top + bias)
            new_max = tops[0]
            for top in tops[1:]:
                new_max = jnp.maximum(new_max, top)
            if not first:
                old_max = run_max[:, cols]
                new_max = jnp.maximum(new_max, old_max)
                alpha = jnp.exp2(old_max - new_max)
            run_max[:, cols] = new_max
            total = None
            pieces = []
            for lo, at, parity, bias in parts:
                shift = -new_max if bias is None else bias - new_max
                piece = jnp.exp2(s[lo:lo + BLOCK] * EXP_SCALE + shift)
                part_sum = jnp.sum(piece, axis=0, keepdims=True)
                total = part_sum if total is None else total + part_sum
                piece = piece.astype(jnp.bfloat16)
                probs[slot, pl.ds(at, BLOCK), cols] = piece
                pieces.append(piece)
                maxes[slot, parity, :, cols] = new_max
            tile = pieces[0] if len(pieces) == 1 else jnp.concatenate(pieces, axis=0)
            mixed = dot_nn(values_t, tile)
            if first:
                run_sum[:, cols] = total
                out_acc[:, cols] = mixed
            else:
                run_sum[:, cols] = run_sum[:, cols] * alpha + total
                out_acc[:, cols] = out_acc[:, cols] * alpha + mixed

    c_rows = pl.multiple_of(c * BLOCK, BLOCK)
    o_rows = pl.multiple_of((1 - c) * BLOCK, BLOCK)
    forward(kv[0, c, 0], kv[0, c, 1].T, 0, [(0, c_rows, c, None)], True)

    x_copy(1).wait_recv()
    p_copy(4).start()
    for k in (1, 2, 3):
        @pl.when(wraps[k] == 0)
        def _():
            y_copy(k, 1).start()

        @pl.when(wraps[k] == 1)
        def _():
            y_copy(k, 0).start()
    x_copy(2).wait_recv()
    special_copy().start()
    for k in (1, 2, 3):
        @pl.when(wraps[k] == 1)
        def _():
            y_copy(k, 1).start()

    g_copy.wait()
    for h in range(HEADS):
        gt[:, head_cols(h)] = g_in[:, head_cols(h)].T

    def arrival(j):
        i = lax.div(j - 1, 2)
        k = 2 * i + 1 - 3 * lax.div(i, 2)
        return jnp.where(j == 0, 4, k + 4 * lax.rem(j + 1, 2))

    def y_wait(e):
        remote(kv.at[e, c], kv.at[e, c], y_send.at[e], x_recv.at[e], partner).wait_recv()

    def forward_step(j, carry):
        e = arrival(j)

        @pl.when(j < 6)
        def _():
            nxt = arrival(j + 1)
            y_wait(nxt)
            p_copy(nxt).start()

        remote(kv.at[e, c], kv.at[e, 1 - c], p_send.at[e], p_recv.at[e], partner).wait_recv()
        keys = kv[e, :, 0].reshape(2 * BLOCK, HEAD_DIM)
        values_t = kv[e, :, 1].reshape(2 * BLOCK, HEAD_DIM).T
        base = p - c - 2 * e
        forward(keys, values_t, e, [(0, 0, 0, bias_of(base)), (BLOCK, BLOCK, 1, bias_of(base + 1))], False)
        return carry

    lax.fori_loop(0, 7, forward_step, 0)

    special_copy().wait_recv()
    special_at = jnp.where(c == 0, p - 15, p - 1)
    forward(kv[0, 1 - c, 0], kv[0, 1 - c, 1].T, 0, [(0, o_rows, 1 - c, bias_of(special_at))], False)

    for h in range(HEADS):
        cols = head_cols(h)
        inv = 1.0 / run_sum[:, cols]
        att_t = (out_acc[:, cols] * inv).astype(jnp.bfloat16)
        att_out[:, cols] = att_t.T
        delta[:, cols] = jnp.sum(
            att_t.astype(jnp.float32) * gt[:, cols].astype(jnp.float32), axis=0, keepdims=True)
        run_sum[:, cols] = inv
    att_copy = pltpu.make_async_copy(att_out, att_hbm, local_sem.at[0])
    att_copy.start()

    dq_acc[...] = jnp.zeros_like(dq_acc)

    def backward(e):
        keys_t = kv[e, :, 0].reshape(2 * BLOCK, HEAD_DIM).T
        values = kv[e, :, 1].reshape(2 * BLOCK, HEAD_DIM)
        for h in range(HEADS):
            cols = head_cols(h)
            gp = dot_nn(values, gt[:, cols]) - delta[:, cols]
            for parity in (0, 1):
                rows = slice(parity * BLOCK, (parity + 1) * BLOCK)
                factor = jnp.exp2(maxes[e, parity, :, cols] - run_max[:, cols]) * run_sum[:, cols]
                w = probs[e, rows, cols].astype(jnp.float32) * factor
                w_scr[rows, cols] = w.astype(jnp.bfloat16)
                ds_scr[rows, cols] = (w * gp[rows]).astype(jnp.bfloat16)
        ds = ds_scr[...]
        dk_t = dot_nt(qt[...], ds)
        dv_t = dot_nt(gt[...], w_scr[...])
        for parity in (0, 1):
            rows = slice(parity * BLOCK, (parity + 1) * BLOCK)
            pg[e, parity, 0] = dk_t[:, rows].astype(jnp.bfloat16)
            pg[e, parity, 1] = dv_t[:, rows].astype(jnp.bfloat16)
        dq_acc[...] += dot_nn(keys_t, ds)

    def r1_copy(e):
        return remote(pg.at[e, 1 - c], r1r.at[e], r1_send.at[e], r1_recv.at[e], partner)

    def r2_copy(e, k):
        return remote(r2s.at[e], r2r.at[e], r2_send.at[e], r2_recv.at[e], y_dev(4 - k))

    def chip_sum(e):
        r1_copy(e).wait_recv()
        return pg[e, c].astype(jnp.float32) + r1r[e].astype(jnp.float32)

    def give_back(j):
        i = lax.div(j, 2)
        k = 2 - i + 3 * lax.div(i, 2)
        return k, k + 4 * lax.rem(j, 2)

    def pass_on(j):
        k, e = give_back(j)
        r2s[e] = chip_sum(e).astype(jnp.bfloat16)
        r2_copy(e, k).start()

    def backward_step(j, carry):
        _, e = give_back(j)
        backward(e)
        r1_copy(e).start()

        @pl.when(j > 0)
        def _():
            pass_on(j - 1)

        return carry

    lax.fori_loop(0, 6, backward_step, 0)
    backward(4)
    r1_copy(4).start()
    pass_on(5)
    backward(0)
    r1_copy(0).start()

    for h in range(HEADS):
        cols = head_cols(h)
        dq_out[:, cols] = (dq_acc[:, cols] * SCALE).astype(jnp.bfloat16).T
    dq_copy = pltpu.make_async_copy(dq_out, dq_hbm, local_sem.at[1])
    dq_copy.start()

    one_back = chip_sum(4)
    own = pg[0, c].astype(jnp.float32)
    two_back = jnp.zeros_like(own)
    r1_copy(0).wait_recv()
    special = r1r[0].astype(jnp.float32)
    own = own + jnp.where(c == 0, special, 0.0)
    two_back = two_back + jnp.where(c == 0, 0.0, special)
    for k in (2, 1, 3):
        r2_copy(k, k).wait_recv()
        near = r2r[k].astype(jnp.float32)
        r2_copy(k + 4, k).wait_recv()
        far = r2r[k + 4].astype(jnp.float32)
        wrapped = wraps[k] == 1
        own = own + jnp.where(wrapped, 0.0, near)
        one_back = one_back + jnp.where(wrapped, near, far)
        two_back = two_back + jnp.where(wrapped, far, 0.0)
    r3s[0] = one_back.astype(jnp.bfloat16)
    r3s[1] = two_back.astype(jnp.bfloat16)

    def r3_copy(i):
        return remote(r3s.at[i], r3r.at[i], r3_send.at[i], r3_recv.at[i], seq_dev(-8 * (i + 1)))

    r3_copy(1).start()
    r3_copy(0).start()

    x_copy(1).wait_send()
    x_copy(2).wait_send()
    special_copy().wait_send()
    for e in range(1, 8):
        p_copy(e).wait_send()
    for k in (1, 2, 3):
        for second in (0, 1):
            y_copy(k, second).wait_send()
            r2_copy(k + 4 * second, k).wait_send()
    for e in range(8):
        r1_copy(e).wait_send()
    att_copy.wait()
    dq_copy.wait()

    r3_copy(0).wait_recv()
    r3_copy(1).wait_recv()
    total = own + r3r[0].astype(jnp.float32) + r3r[1].astype(jnp.float32)
    dkv_out[0] = (total[0] * SCALE).T.astype(jnp.bfloat16)
    dkv_out[1] = total[1].T.astype(jnp.bfloat16)
    dk_copy = pltpu.make_async_copy(dkv_out.at[0], dk_hbm, local_sem.at[2])
    dv_copy = pltpu.make_async_copy(dkv_out.at[1], dv_hbm, local_sem.at[3])
    dk_copy.start()
    dv_copy.start()
    r3_copy(0).wait_send()
    r3_copy(1).wait_send()
    dk_copy.wait()
    dv_copy.wait()


def local(queries, key_rows, value_rows, out_grad, doc_ids):
    bf16, f32 = jnp.bfloat16, jnp.float32
    dma = pltpu.SemaphoreType.DMA
    any_space = pl.BlockSpec(memory_space=pl.ANY)
    pair = (2, BLOCK, HEAD_DIM)
    return pl.pallas_call(
        kernel,
        out_shape=(
            jax.ShapeDtypeStruct((BLOCK, WIDE), bf16),
            jax.ShapeDtypeStruct((BLOCK, WIDE), bf16),
            jax.ShapeDtypeStruct((BLOCK, HEAD_DIM), bf16),
            jax.ShapeDtypeStruct((BLOCK, HEAD_DIM), bf16),
        ),
        in_specs=[any_space] * 5,
        out_specs=(any_space,) * 4,
        scratch_shapes=[
            pltpu.VMEM((9, 2) + pair, bf16),
            pltpu.VMEM((BLOCK, WIDE), bf16),
            pltpu.VMEM((BLOCK, WIDE), bf16),
            pltpu.VMEM((HEAD_DIM, WIDE), bf16),
            pltpu.VMEM((HEAD_DIM, WIDE), bf16),
            pltpu.VMEM((8, 2 * BLOCK, WIDE), bf16),
            pltpu.VMEM((8, 2, 1, WIDE), f32),
            pltpu.VMEM((1, WIDE), f32),
            pltpu.VMEM((1, WIDE), f32),
            pltpu.VMEM((HEAD_DIM, WIDE), f32),
            pltpu.VMEM((HEAD_DIM, WIDE), f32),
            pltpu.VMEM((1, WIDE), f32),
            pltpu.VMEM((2 * BLOCK, WIDE), bf16),
            pltpu.VMEM((2 * BLOCK, WIDE), bf16),
            pltpu.VMEM((8, 2) + pair, bf16),
            pltpu.VMEM((8,) + pair, bf16),
            pltpu.VMEM((8,) + pair, bf16),
            pltpu.VMEM((8,) + pair, bf16),
            pltpu.VMEM((2,) + pair, bf16),
            pltpu.VMEM((2,) + pair, bf16),
            pltpu.VMEM((BLOCK, WIDE), bf16),
            pltpu.VMEM((BLOCK, WIDE), bf16),
            pltpu.VMEM(pair, bf16),
            pltpu.SMEM((NBLK,), jnp.int32),
            dma((4,)),
            dma,
            dma((3,)), dma((9,)), dma((8,)), dma((8,)), dma((8,)),
            dma((8,)), dma((8,)), dma((8,)), dma((8,)), dma((2,)), dma((2,)),
        ],
        compiler_params=pltpu.CompilerParams(collective_id=0, has_side_effects=True),
    )(queries, key_rows, value_rows, out_grad, doc_ids)


def solution(mesh):
    rows = P(("pb", "kv"), None)
    return jax.shard_map(
        local, mesh=mesh, in_specs=(rows, rows, rows, rows, P()),
        out_specs=(rows, rows, rows, rows), check_vma=False)
```

```python
import jax
import jax.numpy as jnp
from jax import lax
from jax.experimental import pallas as pl
from jax.experimental.pallas import tpu as pltpu
from jax.sharding import PartitionSpec as P

HEADS = 8
HEAD_DIM = 128
BLOCK = 128
NBLK = 256
WIDE = HEADS * HEAD_DIM

NEG = -1e30
SCALE = HEAD_DIM ** (-0.5)
LOG2E = 1.4426950408889634
EXP_SCALE = SCALE * LOG2E

MESH = pl.DeviceIdType.MESH
SEND_ORDER = (1, 2, 3, 4, 5, 6, 7)


def dot_nn(a, b):
    return lax.dot_general(a, b, (((1,), (0,)), ((), ())), preferred_element_type=jnp.float32)


def dot_nt(a, b):
    return lax.dot_general(a, b, (((1,), (1,)), ((), ())), preferred_element_type=jnp.float32)


def side_by_side(ref):
    return jnp.concatenate([ref[h] for h in range(HEADS)], axis=1)


def head_cols(h):
    return slice(h * HEAD_DIM, (h + 1) * HEAD_DIM)


def kernel(
    q_hbm, k_hbm, v_hbm, g_hbm, docs_hbm,
    att_out, dq_out, dkv_out,
    kv, q_in, g_in, qt, gt, probs, maxes, run_max, run_sum, out_acc, dq_acc, delta,
    w_scr, ds_scr, pg, r1r, r2s, r2r, r3s, r3b, r3r, total, docs,
    local_sem, q_sem, g_sem, docs_sem,
    kv_send, kv_recv, p_send, p_recv,
    r1_send, r1_recv, r2_send, r2_recv, r3_send, r3_recv,
):
    pb = lax.axis_index("pb")
    kvi = lax.axis_index("kv")
    p = pb * 16 + kvi
    c = lax.rem(kvi, 2)
    y = lax.rem(lax.div(kvi, 2), 4)

    def seq_dev(delta_p):
        t = lax.rem(p + delta_p + NBLK, NBLK)
        return (lax.div(t, 16), lax.rem(t, 16))

    partner = (pb, kvi + 1 - 2 * c)
    chip = lax.div(p, 2)
    column = lax.div(p, 8)

    def there(e):
        return (chip + e >= 0) & (chip + e < NBLK // 2)

    @pl.when(column < 2)
    def _():
        for e in range(1, 9):
            kv[e, c] = jnp.zeros((2, BLOCK, HEAD_DIM), jnp.bfloat16)

    barrier = pltpu.get_barrier_semaphore()
    peers = [e for d in range(1, 9) for e in (d, -d)]
    count = jnp.int32(1)
    pl.semaphore_signal(barrier, inc=1, device_id=partner, device_id_type=MESH)
    for e in peers:
        count = count + there(e).astype(jnp.int32)

        @pl.when(there(e))
        def _():
            pl.semaphore_signal(barrier, inc=1, device_id=seq_dev(2 * e), device_id_type=MESH)

    own_k = pltpu.make_async_copy(k_hbm, kv.at[0, c, 0], local_sem.at[0])
    own_v = pltpu.make_async_copy(v_hbm, kv.at[0, c, 1], local_sem.at[1])
    own_k.start()
    own_v.start()
    docs_copy = pltpu.make_async_copy(docs_hbm, docs, docs_sem)
    docs_copy.start()
    q_copies = [
        pltpu.make_async_copy(q_hbm.at[:, head_cols(h)], q_in.at[h], q_sem.at[h]) for h in range(HEADS)]
    g_copies = [
        pltpu.make_async_copy(g_hbm.at[:, head_cols(h)], g_in.at[h], g_sem.at[h]) for h in range(HEADS)]
    for copy in q_copies + g_copies:
        copy.start()
    own_k.wait()
    own_v.wait()
    pl.semaphore_wait(barrier, count)

    def remote(src, dst, send_sem, recv_sem, dev):
        return pltpu.make_async_remote_copy(
            src_ref=src, dst_ref=dst, send_sem=send_sem, recv_sem=recv_sem,
            device_id=dev, device_id_type=MESH)

    def straight(e):
        return y + e < 8

    def kv_copy(e, passed):
        src = kv.at[8 if passed else 0, c]
        return remote(src, kv.at[e, c], kv_send.at[e], kv_recv.at[e], seq_dev(2 * e - (16 if passed else 0)))

    def kv_wait(e):
        @pl.when(there(-e))
        def _():
            remote(kv.at[0, c], kv.at[e, c], kv_send.at[e], kv_recv.at[e], partner).wait_recv()

    def p_copy(e):
        return remote(kv.at[e, c], kv.at[e, c], p_send.at[e], p_recv.at[e], partner)

    def special_copy():
        return remote(kv.at[8 * c, c], kv.at[0, c], p_send.at[0], p_recv.at[0], partner)

    @pl.when(there(8))
    def _():
        kv_copy(8, False).start()

    for e in SEND_ORDER:
        @pl.when(straight(e) & there(e))
        def _():
            kv_copy(e, False).start()

    for h in range(HEADS):
        q_copies[h].wait()
        qt[h] = q_in[h].T
    docs_copy.wait()
    my_doc = docs[p]

    def bias_of(idx):
        same = (docs[jnp.maximum(idx, 0)] == my_doc) & (idx >= 0)
        return jnp.where(same, 0.0, NEG).astype(jnp.float32)

    def forward(keys, values_t, slot, parts, first):
        for h in range(HEADS):
            cols = head_cols(h)
            s = dot_nn(keys, qt[h])
            if first:
                key_at = lax.broadcasted_iota(jnp.int32, s.shape, 0)
                query_at = lax.broadcasted_iota(jnp.int32, s.shape, 1)
                s = jnp.where(key_at <= query_at, s, NEG)
            tops = []
            for lo, _, _, bias in parts:
                top = jnp.max(s[lo:lo + BLOCK], axis=0, keepdims=True) * EXP_SCALE
                tops.append(top if bias is None else top + bias)
            new_max = tops[0]
            for top in tops[1:]:
                new_max = jnp.maximum(new_max, top)
            if not first:
                old_max = run_max[:, cols]
                new_max = jnp.maximum(new_max, old_max)
                alpha = jnp.exp2(old_max - new_max)
            run_max[:, cols] = new_max
            total = None
            pieces = []
            for lo, at, parity, bias in parts:
                shift = -new_max if bias is None else bias - new_max
                piece = jnp.exp2(s[lo:lo + BLOCK] * EXP_SCALE + shift)
                part_sum = jnp.sum(piece, axis=0, keepdims=True)
                total = part_sum if total is None else total + part_sum
                piece = piece.astype(jnp.bfloat16)
                probs[slot, h, pl.ds(at, BLOCK)] = piece
                pieces.append(piece)
                maxes[slot, parity, :, cols] = new_max
            tile = pieces[0] if len(pieces) == 1 else jnp.concatenate(pieces, axis=0)
            mixed = dot_nn(values_t, tile)
            if first:
                run_sum[:, cols] = total
                out_acc[:, cols] = mixed
            else:
                run_sum[:, cols] = run_sum[:, cols] * alpha + total
                out_acc[:, cols] = out_acc[:, cols] * alpha + mixed

    c_rows = pl.multiple_of(c * BLOCK, BLOCK)
    o_rows = pl.multiple_of((1 - c) * BLOCK, BLOCK)
    forward(kv[0, c, 0], kv[0, c, 1].T, 0, [(0, c_rows, c, None)], True)

    kv_wait(8)
    special_copy().start()
    for e in range(5, 8):
        @pl.when((y + e >= 8) & (column >= 2))
        def _():
            kv_copy(e, True).start()

    kv_wait(1)
    p_copy(1).start()
    for h in range(HEADS):
        g_copies[h].wait()
        gt[h] = g_in[h].T

    def forward_step(e, carry):
        @pl.when(e < 7)
        def _():
            kv_wait(e + 1)
            p_copy(e + 1).start()

        remote(kv.at[e, c], kv.at[e, 1 - c], p_send.at[e], p_recv.at[e], partner).wait_recv()
        keys = kv[e, :, 0].reshape(2 * BLOCK, HEAD_DIM)
        values_t = kv[e, :, 1].reshape(2 * BLOCK, HEAD_DIM).T
        base = p - c - 2 * e
        forward(keys, values_t, e, [(0, 0, 0, bias_of(base)), (BLOCK, BLOCK, 1, bias_of(base + 1))], False)
        return carry

    lax.fori_loop(1, 8, forward_step, 0)

    special_copy().wait_recv()
    special_at = jnp.where(c == 0, p - 15, p - 1)
    forward(kv[0, 1 - c, 0], kv[0, 1 - c, 1].T, 0, [(0, o_rows, 1 - c, bias_of(special_at))], False)

    for h in range(HEADS):
        cols = head_cols(h)
        inv = 1.0 / run_sum[:, cols]
        att_t = (out_acc[:, cols] * inv).astype(jnp.bfloat16)
        att_out[h] = att_t.T
        delta[:, cols] = jnp.sum(
            att_t.astype(jnp.float32) * gt[h].astype(jnp.float32), axis=0, keepdims=True)
        run_sum[:, cols] = inv

    dq_acc[...] = jnp.zeros_like(dq_acc)

    def backward(e):
        keys_t = kv[e, :, 0].reshape(2 * BLOCK, HEAD_DIM).T
        values = kv[e, :, 1].reshape(2 * BLOCK, HEAD_DIM)
        for h in range(HEADS):
            cols = head_cols(h)
            gp = dot_nn(values, gt[h]) - delta[:, cols]
            for parity in (0, 1):
                rows = slice(parity * BLOCK, (parity + 1) * BLOCK)
                factor = jnp.exp2(maxes[e, parity, :, cols] - run_max[:, cols]) * run_sum[:, cols]
                w = probs[e, h, rows].astype(jnp.float32) * factor
                w_scr[h, rows] = w.astype(jnp.bfloat16)
                ds_scr[h, rows] = (w * gp[rows]).astype(jnp.bfloat16)
        ds = side_by_side(ds_scr)
        dk_t = dot_nt(side_by_side(qt), ds)
        dv_t = dot_nt(side_by_side(gt), side_by_side(w_scr))
        for parity in (0, 1):
            rows = slice(parity * BLOCK, (parity + 1) * BLOCK)
            pg[e, parity, 0] = dk_t[:, rows].astype(jnp.bfloat16)
            pg[e, parity, 1] = dv_t[:, rows].astype(jnp.bfloat16)
        dq_acc[...] += dot_nn(keys_t, ds)

    def r1_copy(e):
        return remote(pg.at[e, 1 - c], r1r.at[e], r1_send.at[e], r1_recv.at[e], partner)

    def r2_copy(e):
        passed = jnp.where(e > y + 4, 16, 0)
        return remote(r2s.at[e], r2r.at[e], r2_send.at[e], r2_recv.at[e], seq_dev(passed - 2 * e))

    def chip_sum(e):
        r1_copy(e).wait_recv()
        return pg[e, c].astype(jnp.float32) + r1r[e].astype(jnp.float32)

    def pass_on(e):
        r2s[e] = chip_sum(e).astype(jnp.bfloat16)

        @pl.when(there(-e))
        def _():
            r2_copy(e).start()

    def backward_step(j, carry):
        e = 7 - j
        backward(e)
        r1_copy(e).start()

        @pl.when(j > 0)
        def _():
            pass_on(e + 1)

        return carry

    lax.fori_loop(0, 8, backward_step, 0)

    for h in range(HEADS):
        cols = head_cols(h)
        dq_out[h] = (dq_acc[:, cols] * SCALE).astype(jnp.bfloat16).T

    def r3_copy():
        return remote(r3b, r3r, r3_send, r3_recv, seq_dev(-16))

    own = pg[0, c].astype(jnp.float32)
    r1_copy(0).wait_recv()
    special = r1r[0].astype(jnp.float32)
    own = own + jnp.where(c == 0, special, 0.0)
    r3s[...] = jnp.where(c == 0, 0.0, special)
    for e in range(5, 8):
        @pl.when((y + e >= 8) & (column >= 2))
        def _():
            r2_copy(e).wait_recv()
            r3s[...] += r2r[e].astype(jnp.float32)

    r3b[...] = r3s[...].astype(jnp.bfloat16)

    @pl.when(there(-8))
    def _():
        r3_copy().start()

    total[...] = own
    for e in range(7, 0, -1):
        @pl.when(straight(e) & there(e))
        def _():
            r2_copy(e).wait_recv()
            total[...] += r2r[e].astype(jnp.float32)

    special_copy().wait_send()
    @pl.when(there(8))
    def _():
        kv_copy(8, False).wait_send()

    for e in range(1, 8):
        p_copy(e).wait_send()

        @pl.when(straight(e) & there(e) | (y + e >= 8) & (column >= 2))
        def _():
            kv_copy(e, False).wait_send()

        @pl.when(there(-e))
        def _():
            r2_copy(e).wait_send()

    for e in range(8):
        r1_copy(e).wait_send()


    @pl.when(there(8))
    def _():
        r3_copy().wait_recv()
        total[...] += r3r[...].astype(jnp.float32)

    dkv_out[0] = (total[0] * SCALE).T.astype(jnp.bfloat16)
    dkv_out[1] = total[1].T.astype(jnp.bfloat16)

    @pl.when(there(-8))
    def _():
        r3_copy().wait_send()


def write_out(att, dq, dkv, att_hbm, dq_hbm, dk_hbm, dv_hbm, att_sem, dq_sem, dkv_sem):
    copies = []
    for h in range(HEADS):
        copies.append(pltpu.make_async_copy(att.at[h], att_hbm.at[:, head_cols(h)], att_sem.at[h]))
        copies.append(pltpu.make_async_copy(dq.at[h], dq_hbm.at[:, head_cols(h)], dq_sem.at[h]))
    copies.append(pltpu.make_async_copy(dkv.at[0], dk_hbm, dkv_sem.at[0]))
    copies.append(pltpu.make_async_copy(dkv.at[1], dv_hbm, dkv_sem.at[1]))
    for copy in copies:
        copy.start()
    for copy in copies:
        copy.wait()


def local(queries, key_rows, value_rows, out_grad, doc_ids):
    bf16, f32 = jnp.bfloat16, jnp.float32
    dma = pltpu.SemaphoreType.DMA
    any_space = pl.BlockSpec(memory_space=pl.ANY)
    pair = (2, BLOCK, HEAD_DIM)
    by_head = (HEADS, BLOCK, HEAD_DIM)
    att, dq, dkv = pl.pallas_call(
        kernel,
        out_shape=(pltpu.VMEM(by_head, bf16), pltpu.VMEM(by_head, bf16), pltpu.VMEM(pair, bf16)),
        in_specs=[any_space] * 5,
        out_specs=(pl.BlockSpec(memory_space=pltpu.VMEM),) * 3,
        scratch_shapes=[
            pltpu.VMEM((9, 2) + pair, bf16),
            pltpu.VMEM((HEADS, BLOCK, HEAD_DIM), bf16),
            pltpu.VMEM((HEADS, BLOCK, HEAD_DIM), bf16),
            pltpu.VMEM((HEADS, HEAD_DIM, BLOCK), bf16),
            pltpu.VMEM((HEADS, HEAD_DIM, BLOCK), bf16),
            pltpu.VMEM((8, HEADS, 2 * BLOCK, BLOCK), bf16),
            pltpu.VMEM((8, 2, 1, WIDE), f32),
            pltpu.VMEM((1, WIDE), f32),
            pltpu.VMEM((1, WIDE), f32),
            pltpu.VMEM((HEAD_DIM, WIDE), f32),
            pltpu.VMEM((HEAD_DIM, WIDE), f32),
            pltpu.VMEM((1, WIDE), f32),
            pltpu.VMEM((HEADS, 2 * BLOCK, BLOCK), bf16),
            pltpu.VMEM((HEADS, 2 * BLOCK, BLOCK), bf16),
            pltpu.VMEM((8, 2) + pair, bf16),
            pltpu.VMEM((8,) + pair, bf16),
            pltpu.VMEM((8,) + pair, bf16),
            pltpu.VMEM((8,) + pair, bf16),
            pltpu.VMEM(pair, f32),
            pltpu.VMEM(pair, bf16),
            pltpu.VMEM(pair, bf16),
            pltpu.VMEM(pair, f32),
            pltpu.SMEM((NBLK,), jnp.int32),
            dma((2,)), dma((HEADS,)), dma((HEADS,)),
            dma,
            dma((9,)), dma((9,)), dma((8,)), dma((8,)),
            dma((8,)), dma((8,)), dma((8,)), dma((8,)), dma, dma,
        ],
        compiler_params=pltpu.CompilerParams(collective_id=0, has_side_effects=True),
    )(queries, key_rows, value_rows, out_grad, doc_ids)
    wide = jax.ShapeDtypeStruct((BLOCK, WIDE), bf16)
    narrow = jax.ShapeDtypeStruct((BLOCK, HEAD_DIM), bf16)
    return pl.pallas_call(
        write_out,
        out_shape=(wide, wide, narrow, narrow),
        in_specs=[pl.BlockSpec(memory_space=pltpu.VMEM)] * 3,
        out_specs=(any_space,) * 4,
        scratch_shapes=[dma((HEADS,)), dma((HEADS,)), dma((2,))],
        compiler_params=pltpu.CompilerParams(vmem_limit_bytes=1 << 20),
    )(*[pltpu.with_memory_space_constraint(out, pltpu.VMEM) for out in (att, dq, dkv)])


def solution(mesh):
    rows = P(("pb", "kv"), None)
    return jax.shard_map(
        local, mesh=mesh, in_specs=(rows, rows, rows, rows, P()),
        out_specs=(rows, rows, rows, rows), check_vma=False)
```

```python
import jax
import jax.numpy as jnp
from jax import lax
from jax.experimental import pallas as pl
from jax.experimental.pallas import tpu as pltpu
from jax.sharding import PartitionSpec as P

HEADS = 8
HEAD_DIM = 128
BLOCK = 128
NBLK = 256
WIDE = HEADS * HEAD_DIM

NEG = -1e30
SCALE = HEAD_DIM ** (-0.5)
LOG2E = 1.4426950408889634
EXP_SCALE = SCALE * LOG2E

MESH = pl.DeviceIdType.MESH
SEND_ORDER = (1, 2, 3, 4, 5, 6, 7)


def dot_nn(a, b):
    return lax.dot_general(a, b, (((1,), (0,)), ((), ())), preferred_element_type=jnp.float32)


def dot_nt(a, b):
    return lax.dot_general(a, b, (((1,), (1,)), ((), ())), preferred_element_type=jnp.float32)


def side_by_side(ref):
    return jnp.concatenate([ref[h] for h in range(HEADS)], axis=1)


def head_cols(h):
    return slice(h * HEAD_DIM, (h + 1) * HEAD_DIM)


def kernel(
    q_hbm, k_hbm, v_hbm, g_hbm, docs_hbm,
    att_out, dq_out, dkv_out,
    kv, q_in, g_in, qt, gt, probs, maxes, run_max, run_sum, out_acc, dq_acc, delta,
    w_a, ds_a, w_b, ds_b, ds_all, pg, r1r, r2s, r2r, r3s, r3b, r3r, one_back, r4b, r4r, total, docs,
    local_sem, q_sem, g_sem, docs_sem,
    kv_send, kv_recv, p_send, p_recv,
    r1_send, r1_recv, r2_send, r2_recv, r3_send, r3_recv, r4_send, r4_recv,
):
    pb = lax.axis_index("pb")
    kvi = lax.axis_index("kv")
    p = pb * 16 + kvi
    c = lax.rem(kvi, 2)
    y = lax.rem(lax.div(kvi, 2), 4)

    def seq_dev(delta_p):
        t = lax.rem(p + delta_p + NBLK, NBLK)
        return (lax.div(t, 16), lax.rem(t, 16))

    partner = (pb, kvi + 1 - 2 * c)
    chip = lax.div(p, 2)
    column = lax.div(p, 8)

    def there(e):
        return (chip + e >= 0) & (chip + e < NBLK // 2)

    @pl.when(column < 2)
    def _():
        for e in range(1, 9):
            kv[e, c] = jnp.zeros((2, BLOCK, HEAD_DIM), jnp.bfloat16)

    barrier = pltpu.get_barrier_semaphore()
    peers = [e for d in range(1, 9) for e in (d, -d)]
    count = jnp.int32(1)
    pl.semaphore_signal(barrier, inc=1, device_id=partner, device_id_type=MESH)
    for e in peers:
        count = count + there(e).astype(jnp.int32)

        @pl.when(there(e))
        def _():
            pl.semaphore_signal(barrier, inc=1, device_id=seq_dev(2 * e), device_id_type=MESH)

    own_k = pltpu.make_async_copy(k_hbm, kv.at[0, c, 0], local_sem.at[0])
    own_v = pltpu.make_async_copy(v_hbm, kv.at[0, c, 1], local_sem.at[1])
    own_k.start()
    own_v.start()
    docs_copy = pltpu.make_async_copy(docs_hbm, docs, docs_sem)
    docs_copy.start()
    q_copies = [
        pltpu.make_async_copy(q_hbm.at[:, head_cols(h)], q_in.at[h], q_sem.at[h]) for h in range(HEADS)]
    g_copies = [
        pltpu.make_async_copy(g_hbm.at[:, head_cols(h)], g_in.at[h], g_sem.at[h]) for h in range(HEADS)]
    for copy in q_copies + g_copies:
        copy.start()
    own_k.wait()
    own_v.wait()
    pl.semaphore_wait(barrier, count)

    def remote(src, dst, send_sem, recv_sem, dev):
        return pltpu.make_async_remote_copy(
            src_ref=src, dst_ref=dst, send_sem=send_sem, recv_sem=recv_sem,
            device_id=dev, device_id_type=MESH)

    def straight(e):
        return y + e < 8

    def kv_copy(e, passed):
        src = kv.at[8 if passed else 0, c]
        return remote(src, kv.at[e, c], kv_send.at[e], kv_recv.at[e], seq_dev(2 * e - (16 if passed else 0)))

    def kv_wait(e):
        @pl.when(there(-e))
        def _():
            remote(kv.at[0, c], kv.at[e, c], kv_send.at[e], kv_recv.at[e], partner).wait_recv()

    def p_copy(e):
        return remote(kv.at[e, c], kv.at[e, c], p_send.at[e], p_recv.at[e], partner)

    def special_copy():
        return remote(kv.at[8 * c, c], kv.at[0, c], p_send.at[0], p_recv.at[0], partner)

    two_on = there(8) & ((y > 0) | (c == 1))
    two_back = there(-8) & ((y > 0) | (c == 1))

    def two_wait():
        @pl.when(two_back)
        def _():
            remote(kv.at[0, c], kv.at[8, c], kv_send.at[8], kv_recv.at[8], partner).wait_recv()

    @pl.when(two_on & (y > 0))
    def _():
        kv_copy(8, False).start()

    for e in SEND_ORDER:
        @pl.when(straight(e) & there(e))
        def _():
            kv_copy(e, False).start()

    @pl.when(two_on & (y == 0))
    def _():
        kv_copy(8, False).start()

    @pl.when(c == 0)
    def _():
        special_copy().start()

    for h in range(HEADS):
        q_copies[h].wait()
        qt[h] = q_in[h].T
    docs_copy.wait()
    my_doc = docs[p]

    def bias_of(idx):
        same = (docs[jnp.maximum(idx, 0)] == my_doc) & (idx >= 0)
        return jnp.where(same, 0.0, NEG).astype(jnp.float32)

    def forward(keys, values_t, slot, parts, first):
        for h in range(HEADS):
            cols = head_cols(h)
            s = dot_nn(keys, qt[h])
            if first:
                key_at = lax.broadcasted_iota(jnp.int32, s.shape, 0)
                query_at = lax.broadcasted_iota(jnp.int32, s.shape, 1)
                s = jnp.where(key_at <= query_at, s, NEG)
            tops = []
            for lo, _, _, bias in parts:
                top = jnp.max(s[lo:lo + BLOCK], axis=0, keepdims=True) * EXP_SCALE
                tops.append(top if bias is None else top + bias)
            new_max = tops[0]
            for top in tops[1:]:
                new_max = jnp.maximum(new_max, top)
            if not first:
                old_max = run_max[:, cols]
                new_max = jnp.maximum(new_max, old_max)
                alpha = jnp.exp2(old_max - new_max)
            run_max[:, cols] = new_max
            total = None
            pieces = []
            for lo, at, parity, bias in parts:
                shift = -new_max if bias is None else bias - new_max
                piece = jnp.exp2(s[lo:lo + BLOCK] * EXP_SCALE + shift)
                part_sum = jnp.sum(piece, axis=0, keepdims=True)
                total = part_sum if total is None else total + part_sum
                piece = piece.astype(jnp.bfloat16)
                probs[slot, h, pl.ds(at, BLOCK)] = piece
                pieces.append(piece)
                maxes[slot, parity, :, cols] = new_max
            tile = pieces[0] if len(pieces) == 1 else jnp.concatenate(pieces, axis=0)
            mixed = dot_nn(values_t, tile)
            if first:
                run_sum[:, cols] = total
                out_acc[:, cols] = mixed
            else:
                run_sum[:, cols] = run_sum[:, cols] * alpha + total
                out_acc[:, cols] = out_acc[:, cols] * alpha + mixed

    c_rows = pl.multiple_of(c * BLOCK, BLOCK)
    o_rows = pl.multiple_of((1 - c) * BLOCK, BLOCK)
    forward(kv[0, c, 0], kv[0, c, 1].T, 0, [(0, c_rows, c, None)], True)

    @pl.when(y > 0)
    def _():
        two_wait()

        @pl.when(c == 1)
        def _():
            special_copy().start()

    for e in range(5, 8):
        @pl.when((y + e >= 8) & (column >= 2))
        def _():
            kv_copy(e, True).start()

    for e in (1, 2):
        kv_wait(e)
        p_copy(e).start()
    for h in range(HEADS):
        g_copies[h].wait()
        gt[h] = g_in[h].T

    def forward_step(e, carry):
        @pl.when(e < 6)
        def _():
            kv_wait(e + 2)
            p_copy(e + 2).start()

        @pl.when((e == 5) & (y == 0))
        def _():
            two_wait()

            @pl.when(c == 1)
            def _():
                special_copy().start()

        remote(kv.at[e, c], kv.at[e, 1 - c], p_send.at[e], p_recv.at[e], partner).wait_recv()
        keys = kv[e, :, 0].reshape(2 * BLOCK, HEAD_DIM)
        values_t = kv[e, :, 1].reshape(2 * BLOCK, HEAD_DIM).T
        base = p - c - 2 * e
        forward(keys, values_t, e, [(0, 0, 0, bias_of(base)), (BLOCK, BLOCK, 1, bias_of(base + 1))], False)
        return carry

    lax.fori_loop(1, 8, forward_step, 0)

    special_copy().wait_recv()
    special_at = jnp.where(c == 0, p - 15, p - 1)
    forward(kv[0, 1 - c, 0], kv[0, 1 - c, 1].T, 0, [(0, o_rows, 1 - c, bias_of(special_at))], False)

    for h in range(HEADS):
        cols = head_cols(h)
        inv = 1.0 / run_sum[:, cols]
        att_t = (out_acc[:, cols] * inv).astype(jnp.bfloat16)
        att_out[h] = att_t.T
        delta[:, cols] = jnp.sum(
            att_t.astype(jnp.float32) * gt[h].astype(jnp.float32), axis=0, keepdims=True)
        run_sum[:, cols] = inv

    def weigh(e, w_scr, ds_scr):
        values = kv[e, :, 1].reshape(2 * BLOCK, HEAD_DIM)
        for h in range(HEADS):
            cols = head_cols(h)
            gp = dot_nn(values, gt[h]) - delta[:, cols]
            for parity in (0, 1):
                rows = slice(parity * BLOCK, (parity + 1) * BLOCK)
                factor = jnp.exp2(maxes[e, parity, :, cols] - run_max[:, cols]) * run_sum[:, cols]
                w = probs[e, h, rows].astype(jnp.float32) * factor
                w_scr[h, rows] = w.astype(jnp.bfloat16)
                ds = (w * gp[rows]).astype(jnp.bfloat16)
                ds_scr[h, rows] = ds
                ds_all[e, h, rows] = ds

    def products(e, w_scr, ds_scr):
        dk_t = dot_nt(side_by_side(qt), side_by_side(ds_scr))
        dv_t = dot_nt(side_by_side(gt), side_by_side(w_scr))
        for parity in (0, 1):
            rows = slice(parity * BLOCK, (parity + 1) * BLOCK)
            pg[e, parity, 0] = dk_t[:, rows].astype(jnp.bfloat16)
            pg[e, parity, 1] = dv_t[:, rows].astype(jnp.bfloat16)

    def r1_copy(e):
        return remote(pg.at[e, 1 - c], r1r.at[e], r1_send.at[e], r1_recv.at[e], partner)

    def r3_copy():
        return remote(r3b, r3r, r3_send, r3_recv, seq_dev(-16))

    def beside(e):
        return (e == 3) & (y < 3) | (e == 5) & (y > 0) | (e == 7) & (y == 3) | (e == 1) & (y == 0)

    def r2_copy(e):
        passed = jnp.where(beside(e), 8, jnp.where(e > y + 4, 16, 0))
        return remote(r2s.at[e], r2r.at[e], r2_send.at[e], r2_recv.at[e], seq_dev(passed - 2 * e))

    def chip_sum(e):
        r1_copy(e).wait_recv()
        return pg[e, c].astype(jnp.float32) + r1r[e].astype(jnp.float32)

    def r4_copy():
        return remote(r4b, r4r, r4_send, r4_recv, seq_dev(-8))

    def pass_on(e):
        @pl.when(e != 4)
        def _():
            r2s[e] = chip_sum(e).astype(jnp.bfloat16)

            @pl.when(there(-e))
            def _():
                r2_copy(e).start()

    orders = [(0, 3, 1, 7, 6, 5, 4, 2), (0, 3, 5, 7, 6, 4, 2, 1), (0, 3, 5, 7, 4, 6, 2, 1), (0, 5, 7, 4, 6, 2, 3, 1)]
    codes = [sum(e << (3 * j) for j, e in enumerate(order)) for order in orders]
    turns = jnp.where(y == 0, codes[0], jnp.where(y == 1, codes[1], jnp.where(y == 2, codes[2], codes[3])))

    def turn(j):
        return lax.rem(lax.shift_right_logical(turns, 3 * jnp.asarray(j, jnp.int32)), 8)

    later_sum = y > 0
    beside_in = {1: y == 3, 3: y > 0, 5: y < 3, 7: y == 0}
    straight_in = {
        e: (y + e < 4) | there(e) & ((e == 6) & (y < 2) | (e == 2) & (y > 1)) for e in (1, 2, 3, 6)}
    r3_sent = there(-8) & ((y > 0) | (c == 1))
    r3_due = there(8) & ((y > 0) | (c == 1))

    def hand_over(j):
        r1_copy(turn(j)).start()

        @pl.when(j > 2)
        def _():
            pass_on(turn(j - 2))

        @pl.when((j == 2) & ~later_sum)
        def _():
            r1_copy(0).wait_recv()
            special = r1r[0].astype(jnp.float32)
            total[...] = pg[0, c].astype(jnp.float32) + jnp.where(c == 0, special, 0.0)

            @pl.when(there(-8) & (c == 1))
            def _():
                r3b[...] = r1r[0]
                r3_copy().start()

    weigh(turn(0), w_a, ds_a)

    def backward_steps(i, carry):
        j = 2 * i
        weigh(turn(j + 1), w_b, ds_b)
        products(turn(j), w_a, ds_a)
        hand_over(j)
        weigh(turn(j + 2), w_a, ds_a)
        products(turn(j + 1), w_b, ds_b)
        hand_over(j + 1)
        return carry

    lax.fori_loop(0, 3, backward_steps, 0)
    weigh(turn(7), w_b, ds_b)
    products(turn(6), w_a, ds_a)
    hand_over(jnp.int32(6))
    products(turn(7), w_b, ds_b)
    hand_over(jnp.int32(7))
    pass_on(turn(6))
    pass_on(turn(7))

    one_back[...] = chip_sum(4)
    for e in (1, 3, 5, 7):
        @pl.when(beside_in[e] & (column >= 1))
        def _():
            r2_copy(e).wait_recv()
            one_back[...] += r2r[e].astype(jnp.float32)

    @pl.when(there(-4))
    def _():
        r4b[...] = one_back[...].astype(jnp.bfloat16)
        r4_copy().start()

    @pl.when(later_sum)
    def _():
        r1_copy(0).wait_recv()
        special = r1r[0].astype(jnp.float32)
        total[...] = pg[0, c].astype(jnp.float32) + jnp.where(c == 0, special, 0.0)
        r3s[...] = jnp.where(c == 0, 0.0, special)

    for e in range(5, 8):
        @pl.when((y + e >= 8) & (column >= 2))
        def _():
            r2_copy(e).wait_recv()
            r3s[...] += r2r[e].astype(jnp.float32)

    @pl.when(there(-8) & (y > 0))
    def _():
        r3b[...] = r3s[...].astype(jnp.bfloat16)
        r3_copy().start()

    def query_grads(e, carry):
        keys_t = kv[e, :, 0].reshape(2 * BLOCK, HEAD_DIM).T
        dq_acc[...] += dot_nn(keys_t, side_by_side(ds_all.at[e]))
        return carry

    dq_acc[...] = dot_nn(kv[0, :, 0].reshape(2 * BLOCK, HEAD_DIM).T, side_by_side(ds_all.at[0]))
    lax.fori_loop(1, 8, query_grads, 0)
    for h in range(HEADS):
        dq_out[h] = (dq_acc[:, head_cols(h)] * SCALE).astype(jnp.bfloat16).T

    for e in (6, 3, 2, 1):
        @pl.when(straight_in[e])
        def _():
            r2_copy(e).wait_recv()
            total[...] += r2r[e].astype(jnp.float32)

    special_copy().wait_send()
    @pl.when(two_on)
    def _():
        kv_copy(8, False).wait_send()

    for e in range(1, 8):
        p_copy(e).wait_send()

        @pl.when(straight(e) & there(e) | (y + e >= 8) & (column >= 2))
        def _():
            kv_copy(e, False).wait_send()

        if e != 4:
            @pl.when(there(-e))
            def _():
                r2_copy(e).wait_send()

    for e in range(8):
        r1_copy(e).wait_send()


    @pl.when(there(4))
    def _():
        r4_copy().wait_recv()
        total[...] += r4r[...].astype(jnp.float32)

    @pl.when(r3_due)
    def _():
        r3_copy().wait_recv()
        total[...] += r3r[...].astype(jnp.float32)

    dkv_out[0] = (total[0] * SCALE).T.astype(jnp.bfloat16)
    dkv_out[1] = total[1].T.astype(jnp.bfloat16)

    @pl.when(r3_sent)
    def _():
        r3_copy().wait_send()

    @pl.when(there(-4))
    def _():
        r4_copy().wait_send()


def write_out(att, dq, dkv, att_hbm, dq_hbm, dk_hbm, dv_hbm, att_sem, dq_sem, dkv_sem):
    copies = []
    for h in range(HEADS):
        copies.append(pltpu.make_async_copy(att.at[h], att_hbm.at[:, head_cols(h)], att_sem.at[h]))
        copies.append(pltpu.make_async_copy(dq.at[h], dq_hbm.at[:, head_cols(h)], dq_sem.at[h]))
    copies.append(pltpu.make_async_copy(dkv.at[0], dk_hbm, dkv_sem.at[0]))
    copies.append(pltpu.make_async_copy(dkv.at[1], dv_hbm, dkv_sem.at[1]))
    for copy in copies:
        copy.start()
    for copy in copies:
        copy.wait()


def local(queries, key_rows, value_rows, out_grad, doc_ids):
    bf16, f32 = jnp.bfloat16, jnp.float32
    dma = pltpu.SemaphoreType.DMA
    any_space = pl.BlockSpec(memory_space=pl.ANY)
    pair = (2, BLOCK, HEAD_DIM)
    by_head = (HEADS, BLOCK, HEAD_DIM)
    att, dq, dkv = pl.pallas_call(
        kernel,
        out_shape=(pltpu.VMEM(by_head, bf16), pltpu.VMEM(by_head, bf16), pltpu.VMEM(pair, bf16)),
        in_specs=[any_space] * 5,
        out_specs=(pl.BlockSpec(memory_space=pltpu.VMEM),) * 3,
        scratch_shapes=[
            pltpu.VMEM((9, 2) + pair, bf16),
            pltpu.VMEM((HEADS, BLOCK, HEAD_DIM), bf16),
            pltpu.VMEM((HEADS, BLOCK, HEAD_DIM), bf16),
            pltpu.VMEM((HEADS, HEAD_DIM, BLOCK), bf16),
            pltpu.VMEM((HEADS, HEAD_DIM, BLOCK), bf16),
            pltpu.VMEM((8, HEADS, 2 * BLOCK, BLOCK), bf16),
            pltpu.VMEM((8, 2, 1, WIDE), f32),
            pltpu.VMEM((1, WIDE), f32),
            pltpu.VMEM((1, WIDE), f32),
            pltpu.VMEM((HEAD_DIM, WIDE), f32),
            pltpu.VMEM((HEAD_DIM, WIDE), f32),
            pltpu.VMEM((1, WIDE), f32),
            pltpu.VMEM((HEADS, 2 * BLOCK, BLOCK), bf16),
            pltpu.VMEM((HEADS, 2 * BLOCK, BLOCK), bf16),
            pltpu.VMEM((HEADS, 2 * BLOCK, BLOCK), bf16),
            pltpu.VMEM((HEADS, 2 * BLOCK, BLOCK), bf16),
            pltpu.VMEM((8, HEADS, 2 * BLOCK, BLOCK), bf16),
            pltpu.VMEM((8, 2) + pair, bf16),
            pltpu.VMEM((8,) + pair, bf16),
            pltpu.VMEM((8,) + pair, bf16),
            pltpu.VMEM((8,) + pair, bf16),
            pltpu.VMEM(pair, f32),
            pltpu.VMEM(pair, bf16),
            pltpu.VMEM(pair, bf16),
            pltpu.VMEM(pair, f32),
            pltpu.VMEM(pair, bf16),
            pltpu.VMEM(pair, bf16),
            pltpu.VMEM(pair, f32),
            pltpu.SMEM((NBLK,), jnp.int32),
            dma((2,)), dma((HEADS,)), dma((HEADS,)),
            dma,
            dma((9,)), dma((9,)), dma((8,)), dma((8,)),
            dma((8,)), dma((8,)), dma((8,)), dma((8,)), dma, dma, dma, dma,
        ],
        compiler_params=pltpu.CompilerParams(collective_id=0, has_side_effects=True),
    )(queries, key_rows, value_rows, out_grad, doc_ids)
    wide = jax.ShapeDtypeStruct((BLOCK, WIDE), bf16)
    narrow = jax.ShapeDtypeStruct((BLOCK, HEAD_DIM), bf16)
    return pl.pallas_call(
        write_out,
        out_shape=(wide, wide, narrow, narrow),
        in_specs=[pl.BlockSpec(memory_space=pltpu.VMEM)] * 3,
        out_specs=(any_space,) * 4,
        scratch_shapes=[dma((HEADS,)), dma((HEADS,)), dma((2,))],
        compiler_params=pltpu.CompilerParams(vmem_limit_bytes=1 << 20),
    )(*[pltpu.with_memory_space_constraint(out, pltpu.VMEM) for out in (att, dq, dkv)])


def solution(mesh):
    rows = P(("pb", "kv"), None)
    return jax.shard_map(
        local, mesh=mesh, in_specs=(rows, rows, rows, rows, P()),
        out_specs=(rows, rows, rows, rows), check_vma=False)
```

```python
import jax
import jax.numpy as jnp
from jax import lax
from jax.experimental import pallas as pl
from jax.experimental.pallas import tpu as pltpu
from jax.sharding import PartitionSpec as P

HEADS = 8
HEAD_DIM = 128
BLOCK = 128
NBLK = 256
WIDE = HEADS * HEAD_DIM

NEG = -1e30
SCALE = HEAD_DIM ** (-0.5)
LOG2E = 1.4426950408889634
EXP_SCALE = SCALE * LOG2E

MESH = pl.DeviceIdType.MESH
SEND_ORDER = (1, 2, 3, 4, 5, 6, 7)


def dot_nn(a, b):
    return lax.dot_general(a, b, (((1,), (0,)), ((), ())), preferred_element_type=jnp.float32)


def dot_nt(a, b):
    return lax.dot_general(a, b, (((1,), (1,)), ((), ())), preferred_element_type=jnp.float32)


def side_by_side(ref):
    return jnp.concatenate([ref[h] for h in range(HEADS)], axis=1)


def head_cols(h):
    return slice(h * HEAD_DIM, (h + 1) * HEAD_DIM)


def kernel(
    q_hbm, k_hbm, v_hbm, g_hbm, docs_hbm,
    att_out, dq_out, dkv_out,
    kv, q_in, g_in, qt, gt, probs, maxes, run_max, run_sum, out_acc, dq_acc, delta,
    w_a, ds_a, w_b, ds_b, ds_all, pg, r1r, r2s, r2r, r3s, r3b, r3r, one_back, r4b, r4r, total, docs,
    local_sem, q_sem, g_sem, docs_sem,
    kv_send, kv_recv, p_send, p_recv,
    r1_send, r1_recv, r2_send, r2_recv, r3_send, r3_recv, r4_send, r4_recv,
):
    pb = lax.axis_index("pb")
    kvi = lax.axis_index("kv")
    p = pb * 16 + kvi
    c = lax.rem(kvi, 2)
    y = lax.rem(lax.div(kvi, 2), 4)

    def seq_dev(delta_p):
        t = lax.rem(p + delta_p + NBLK, NBLK)
        return (lax.div(t, 16), lax.rem(t, 16))

    partner = (pb, kvi + 1 - 2 * c)
    chip = lax.div(p, 2)
    column = lax.div(p, 8)

    def there(e):
        return (chip + e >= 0) & (chip + e < NBLK // 2)

    @pl.when(column < 2)
    def _():
        for e in range(1, 9):
            kv[e, c] = jnp.zeros((2, BLOCK, HEAD_DIM), jnp.bfloat16)

    barrier = pltpu.get_barrier_semaphore()
    peers = [e for d in range(1, 9) for e in (d, -d)]
    count = jnp.int32(1)
    pl.semaphore_signal(barrier, inc=1, device_id=partner, device_id_type=MESH)
    for e in peers:
        count = count + there(e).astype(jnp.int32)

        @pl.when(there(e))
        def _():
            pl.semaphore_signal(barrier, inc=1, device_id=seq_dev(2 * e), device_id_type=MESH)

    own_k = pltpu.make_async_copy(k_hbm, kv.at[0, c, 0], local_sem.at[0])
    own_v = pltpu.make_async_copy(v_hbm, kv.at[0, c, 1], local_sem.at[1])
    own_k.start()
    own_v.start()
    docs_copy = pltpu.make_async_copy(docs_hbm, docs, docs_sem)
    docs_copy.start()
    q_copies = [
        pltpu.make_async_copy(q_hbm.at[:, head_cols(h)], q_in.at[h], q_sem.at[h]) for h in range(HEADS)]
    g_copies = [
        pltpu.make_async_copy(g_hbm.at[:, head_cols(h)], g_in.at[h], g_sem.at[h]) for h in range(HEADS)]
    for copy in q_copies + g_copies:
        copy.start()
    own_k.wait()
    own_v.wait()
    pl.semaphore_wait(barrier, count)

    def remote(src, dst, send_sem, recv_sem, dev):
        return pltpu.make_async_remote_copy(
            src_ref=src, dst_ref=dst, send_sem=send_sem, recv_sem=recv_sem,
            device_id=dev, device_id_type=MESH)

    def straight(e):
        return y + e < 8

    def kv_copy(e, passed):
        src = kv.at[8 if passed else 0, c]
        return remote(src, kv.at[e, c], kv_send.at[e], kv_recv.at[e], seq_dev(2 * e - (16 if passed else 0)))

    def kv_wait(e):
        @pl.when(there(-e))
        def _():
            remote(kv.at[0, c], kv.at[e, c], kv_send.at[e], kv_recv.at[e], partner).wait_recv()

    def p_copy(e):
        return remote(kv.at[e, c], kv.at[e, c], p_send.at[e], p_recv.at[e], partner)

    def special_copy():
        return remote(kv.at[8 * c, c], kv.at[0, c], p_send.at[0], p_recv.at[0], partner)

    two_on = there(8) & ((y > 0) | (c == 1))
    two_back = there(-8) & ((y > 0) | (c == 1))

    def two_wait():
        @pl.when(two_back)
        def _():
            remote(kv.at[0, c], kv.at[8, c], kv_send.at[8], kv_recv.at[8], partner).wait_recv()

    @pl.when(two_on & (y > 0))
    def _():
        kv_copy(8, False).start()

    for e in SEND_ORDER:
        @pl.when(straight(e) & there(e))
        def _():
            kv_copy(e, False).start()

    @pl.when(two_on & (y == 0))
    def _():
        kv_copy(8, False).start()

    @pl.when(c == 0)
    def _():
        special_copy().start()

    for h in range(HEADS):
        q_copies[h].wait()
        qt[h] = q_in[h].T
    docs_copy.wait()
    my_doc = docs[p]

    def bias_of(idx):
        same = (docs[jnp.maximum(idx, 0)] == my_doc) & (idx >= 0)
        return jnp.where(same, 0.0, NEG).astype(jnp.float32)

    def forward(keys, values_t, slot, parts, first):
        for h in range(HEADS):
            cols = head_cols(h)
            s = dot_nn(keys, qt[h])
            if first:
                key_at = lax.broadcasted_iota(jnp.int32, s.shape, 0)
                query_at = lax.broadcasted_iota(jnp.int32, s.shape, 1)
                s = jnp.where(key_at <= query_at, s, NEG)
            tops = []
            for lo, _, _, bias in parts:
                top = jnp.max(s[lo:lo + BLOCK], axis=0, keepdims=True) * EXP_SCALE
                tops.append(top if bias is None else top + bias)
            new_max = tops[0]
            for top in tops[1:]:
                new_max = jnp.maximum(new_max, top)
            if not first:
                old_max = run_max[:, cols]
                new_max = jnp.maximum(new_max, old_max)
                alpha = jnp.exp2(old_max - new_max)
            run_max[:, cols] = new_max
            total = None
            pieces = []
            for lo, at, parity, bias in parts:
                shift = -new_max if bias is None else bias - new_max
                piece = jnp.exp2(s[lo:lo + BLOCK] * EXP_SCALE + shift)
                part_sum = jnp.sum(piece, axis=0, keepdims=True)
                total = part_sum if total is None else total + part_sum
                piece = piece.astype(jnp.bfloat16)
                probs[slot, h, pl.ds(at, BLOCK)] = piece
                pieces.append(piece)
                maxes[slot, parity, :, cols] = new_max
            tile = pieces[0] if len(pieces) == 1 else jnp.concatenate(pieces, axis=0)
            mixed = dot_nn(values_t, tile)
            if first:
                run_sum[:, cols] = total
                out_acc[:, cols] = mixed
            else:
                run_sum[:, cols] = run_sum[:, cols] * alpha + total
                out_acc[:, cols] = out_acc[:, cols] * alpha + mixed

    c_rows = pl.multiple_of(c * BLOCK, BLOCK)
    o_rows = pl.multiple_of((1 - c) * BLOCK, BLOCK)
    forward(kv[0, c, 0], kv[0, c, 1].T, 0, [(0, c_rows, c, None)], True)

    @pl.when(y > 0)
    def _():
        two_wait()

        @pl.when(c == 1)
        def _():
            special_copy().start()

    for e in range(5, 8):
        @pl.when((y + e >= 8) & (column >= 2))
        def _():
            kv_copy(e, True).start()

    for e in (1, 2):
        kv_wait(e)
        p_copy(e).start()
    for h in range(HEADS):
        g_copies[h].wait()
        gt[h] = g_in[h].T

    def forward_step(e, carry):
        @pl.when(e < 6)
        def _():
            kv_wait(e + 2)
            p_copy(e + 2).start()

        @pl.when((e == 5) & (y == 0))
        def _():
            two_wait()

            @pl.when(c == 1)
            def _():
                special_copy().start()

        remote(kv.at[e, c], kv.at[e, 1 - c], p_send.at[e], p_recv.at[e], partner).wait_recv()
        keys = kv[e, :, 0].reshape(2 * BLOCK, HEAD_DIM)
        values_t = kv[e, :, 1].reshape(2 * BLOCK, HEAD_DIM).T
        base = p - c - 2 * e
        forward(keys, values_t, e, [(0, 0, 0, bias_of(base)), (BLOCK, BLOCK, 1, bias_of(base + 1))], False)
        return carry

    lax.fori_loop(1, 8, forward_step, 0)

    special_copy().wait_recv()
    special_at = jnp.where(c == 0, p - 15, p - 1)
    forward(kv[0, 1 - c, 0], kv[0, 1 - c, 1].T, 0, [(0, o_rows, 1 - c, bias_of(special_at))], False)

    for h in range(HEADS):
        cols = head_cols(h)
        inv = 1.0 / run_sum[:, cols]
        att_t = (out_acc[:, cols] * inv).astype(jnp.bfloat16)
        att_out[h] = att_t.T
        delta[:, cols] = jnp.sum(
            att_t.astype(jnp.float32) * gt[h].astype(jnp.float32), axis=0, keepdims=True)
        run_sum[:, cols] = inv

    def weigh(e, w_scr, ds_scr):
        values = kv[e, :, 1].reshape(2 * BLOCK, HEAD_DIM)
        for h in range(HEADS):
            cols = head_cols(h)
            gp = dot_nn(values, gt[h]) - delta[:, cols]
            for parity in (0, 1):
                rows = slice(parity * BLOCK, (parity + 1) * BLOCK)
                factor = jnp.exp2(maxes[e, parity, :, cols] - run_max[:, cols]) * run_sum[:, cols]
                w = probs[e, h, rows].astype(jnp.float32) * factor
                w_scr[h, rows] = w.astype(jnp.bfloat16)
                ds = (w * gp[rows]).astype(jnp.bfloat16)
                ds_scr[h, rows] = ds
                ds_all[e, h, rows] = ds

    def products(e, w_scr, ds_scr):
        dk_t = dot_nt(side_by_side(qt), side_by_side(ds_scr))
        dv_t = dot_nt(side_by_side(gt), side_by_side(w_scr))
        for parity in (0, 1):
            rows = slice(parity * BLOCK, (parity + 1) * BLOCK)
            pg[e, parity, 0] = dk_t[:, rows].astype(jnp.bfloat16)
            pg[e, parity, 1] = dv_t[:, rows].astype(jnp.bfloat16)

    def r1_copy(e):
        return remote(pg.at[e, 1 - c], r1r.at[e], r1_send.at[e], r1_recv.at[e], partner)

    def r3_copy():
        return remote(r3b, r3r, r3_send, r3_recv, seq_dev(-16))

    def beside(e):
        return (e == 3) & (y < 3) | (e == 5) & (y > 0) | (e == 7) & (y == 3) | (e == 1) & (y == 0)

    def r2_copy(e):
        passed = jnp.where(beside(e), 8, jnp.where(e > y + 4, 16, 0))
        return remote(r2s.at[e], r2r.at[e], r2_send.at[e], r2_recv.at[e], seq_dev(passed - 2 * e))

    def chip_sum(e):
        r1_copy(e).wait_recv()
        return pg[e, c].astype(jnp.float32) + r1r[e].astype(jnp.float32)

    def r4_copy():
        return remote(r4b, r4r, r4_send, r4_recv, seq_dev(-8))

    def pass_on(e):
        @pl.when(e != 4)
        def _():
            r2s[e] = chip_sum(e).astype(jnp.bfloat16)

            @pl.when(there(-e))
            def _():
                r2_copy(e).start()

    orders = [(0, 3, 1, 2, 7, 6, 5, 4), (0, 3, 5, 2, 7, 6, 4, 1), (0, 3, 5, 6, 7, 4, 2, 1), (0, 5, 7, 6, 4, 2, 3, 1)]
    codes = [sum(e << (3 * j) for j, e in enumerate(order)) for order in orders]
    turns = jnp.where(y == 0, codes[0], jnp.where(y == 1, codes[1], jnp.where(y == 2, codes[2], codes[3])))

    def turn(j):
        return lax.rem(lax.shift_right_logical(turns, 3 * jnp.asarray(j, jnp.int32)), 8)

    later_sum = y > 0
    beside_in = {1: y == 3, 3: y > 0, 5: y < 3, 7: y == 0}
    straight_in = {
        e: (y + e < 4) | there(e) & ((e == 6) & (y < 2) | (e == 2) & (y > 1)) for e in (1, 2, 3, 6)}
    r3_sent = there(-8) & ((y > 0) | (c == 1))
    r3_due = there(8) & ((y > 0) | (c == 1))

    def hand_over(j):
        r1_copy(turn(j)).start()

        @pl.when(j > 2)
        def _():
            pass_on(turn(j - 2))

        @pl.when((j == 2) & ~later_sum)
        def _():
            r1_copy(0).wait_recv()
            special = r1r[0].astype(jnp.float32)
            total[...] = pg[0, c].astype(jnp.float32) + jnp.where(c == 0, special, 0.0)

            @pl.when(there(-8) & (c == 1))
            def _():
                r3b[...] = r1r[0]
                r3_copy().start()

    weigh(turn(0), w_a, ds_a)

    def backward_steps(i, carry):
        j = 2 * i
        weigh(turn(j + 1), w_b, ds_b)
        products(turn(j), w_a, ds_a)
        hand_over(j)
        weigh(turn(j + 2), w_a, ds_a)
        products(turn(j + 1), w_b, ds_b)
        hand_over(j + 1)
        return carry

    lax.fori_loop(0, 3, backward_steps, 0)
    weigh(turn(7), w_b, ds_b)
    products(turn(6), w_a, ds_a)
    hand_over(jnp.int32(6))
    products(turn(7), w_b, ds_b)
    hand_over(jnp.int32(7))
    pass_on(turn(6))
    pass_on(turn(7))

    one_back[...] = chip_sum(4)
    for e in (1, 3, 5, 7):
        @pl.when(beside_in[e] & (column >= 1))
        def _():
            r2_copy(e).wait_recv()
            one_back[...] += r2r[e].astype(jnp.float32)

    @pl.when(there(-4))
    def _():
        r4b[...] = one_back[...].astype(jnp.bfloat16)
        r4_copy().start()

    @pl.when(later_sum)
    def _():
        r1_copy(0).wait_recv()
        special = r1r[0].astype(jnp.float32)
        total[...] = pg[0, c].astype(jnp.float32) + jnp.where(c == 0, special, 0.0)
        r3s[...] = jnp.where(c == 0, 0.0, special)

    for e in range(5, 8):
        @pl.when((y + e >= 8) & (column >= 2))
        def _():
            r2_copy(e).wait_recv()
            r3s[...] += r2r[e].astype(jnp.float32)

    @pl.when(there(-8) & (y > 0))
    def _():
        r3b[...] = r3s[...].astype(jnp.bfloat16)
        r3_copy().start()

    def query_grads(e, carry):
        keys_t = kv[e, :, 0].reshape(2 * BLOCK, HEAD_DIM).T
        dq_acc[...] += dot_nn(keys_t, side_by_side(ds_all.at[e]))
        return carry

    dq_acc[...] = dot_nn(kv[0, :, 0].reshape(2 * BLOCK, HEAD_DIM).T, side_by_side(ds_all.at[0]))
    lax.fori_loop(1, 8, query_grads, 0)
    for h in range(HEADS):
        dq_out[h] = (dq_acc[:, head_cols(h)] * SCALE).astype(jnp.bfloat16).T

    for e in (6, 3, 2, 1):
        @pl.when(straight_in[e])
        def _():
            r2_copy(e).wait_recv()
            total[...] += r2r[e].astype(jnp.float32)

    special_copy().wait_send()
    @pl.when(two_on)
    def _():
        kv_copy(8, False).wait_send()

    for e in range(1, 8):
        p_copy(e).wait_send()

        @pl.when(straight(e) & there(e) | (y + e >= 8) & (column >= 2))
        def _():
            kv_copy(e, False).wait_send()

        if e != 4:
            @pl.when(there(-e))
            def _():
                r2_copy(e).wait_send()

    for e in range(8):
        r1_copy(e).wait_send()


    @pl.when(there(4))
    def _():
        r4_copy().wait_recv()
        total[...] += r4r[...].astype(jnp.float32)

    @pl.when(r3_due)
    def _():
        r3_copy().wait_recv()
        total[...] += r3r[...].astype(jnp.float32)

    dkv_out[0] = (total[0] * SCALE).T.astype(jnp.bfloat16)
    dkv_out[1] = total[1].T.astype(jnp.bfloat16)

    @pl.when(r3_sent)
    def _():
        r3_copy().wait_send()

    @pl.when(there(-4))
    def _():
        r4_copy().wait_send()


def write_out(att, dq, dkv, att_hbm, dq_hbm, dk_hbm, dv_hbm, att_sem, dq_sem, dkv_sem):
    copies = []
    for h in range(HEADS):
        copies.append(pltpu.make_async_copy(att.at[h], att_hbm.at[:, head_cols(h)], att_sem.at[h]))
        copies.append(pltpu.make_async_copy(dq.at[h], dq_hbm.at[:, head_cols(h)], dq_sem.at[h]))
    copies.append(pltpu.make_async_copy(dkv.at[0], dk_hbm, dkv_sem.at[0]))
    copies.append(pltpu.make_async_copy(dkv.at[1], dv_hbm, dkv_sem.at[1]))
    for copy in copies:
        copy.start()
    for copy in copies:
        copy.wait()


def local(queries, key_rows, value_rows, out_grad, doc_ids):
    bf16, f32 = jnp.bfloat16, jnp.float32
    dma = pltpu.SemaphoreType.DMA
    any_space = pl.BlockSpec(memory_space=pl.ANY)
    pair = (2, BLOCK, HEAD_DIM)
    by_head = (HEADS, BLOCK, HEAD_DIM)
    att, dq, dkv = pl.pallas_call(
        kernel,
        out_shape=(pltpu.VMEM(by_head, bf16), pltpu.VMEM(by_head, bf16), pltpu.VMEM(pair, bf16)),
        in_specs=[any_space] * 5,
        out_specs=(pl.BlockSpec(memory_space=pltpu.VMEM),) * 3,
        scratch_shapes=[
            pltpu.VMEM((9, 2) + pair, bf16),
            pltpu.VMEM((HEADS, BLOCK, HEAD_DIM), bf16),
            pltpu.VMEM((HEADS, BLOCK, HEAD_DIM), bf16),
            pltpu.VMEM((HEADS, HEAD_DIM, BLOCK), bf16),
            pltpu.VMEM((HEADS, HEAD_DIM, BLOCK), bf16),
            pltpu.VMEM((8, HEADS, 2 * BLOCK, BLOCK), bf16),
            pltpu.VMEM((8, 2, 1, WIDE), f32),
            pltpu.VMEM((1, WIDE), f32),
            pltpu.VMEM((1, WIDE), f32),
            pltpu.VMEM((HEAD_DIM, WIDE), f32),
            pltpu.VMEM((HEAD_DIM, WIDE), f32),
            pltpu.VMEM((1, WIDE), f32),
            pltpu.VMEM((HEADS, 2 * BLOCK, BLOCK), bf16),
            pltpu.VMEM((HEADS, 2 * BLOCK, BLOCK), bf16),
            pltpu.VMEM((HEADS, 2 * BLOCK, BLOCK), bf16),
            pltpu.VMEM((HEADS, 2 * BLOCK, BLOCK), bf16),
            pltpu.VMEM((8, HEADS, 2 * BLOCK, BLOCK), bf16),
            pltpu.VMEM((8, 2) + pair, bf16),
            pltpu.VMEM((8,) + pair, bf16),
            pltpu.VMEM((8,) + pair, bf16),
            pltpu.VMEM((8,) + pair, bf16),
            pltpu.VMEM(pair, f32),
            pltpu.VMEM(pair, bf16),
            pltpu.VMEM(pair, bf16),
            pltpu.VMEM(pair, f32),
            pltpu.VMEM(pair, bf16),
            pltpu.VMEM(pair, bf16),
            pltpu.VMEM(pair, f32),
            pltpu.SMEM((NBLK,), jnp.int32),
            dma((2,)), dma((HEADS,)), dma((HEADS,)),
            dma,
            dma((9,)), dma((9,)), dma((8,)), dma((8,)),
            dma((8,)), dma((8,)), dma((8,)), dma((8,)), dma, dma, dma, dma,
        ],
        compiler_params=pltpu.CompilerParams(collective_id=0, has_side_effects=True),
    )(queries, key_rows, value_rows, out_grad, doc_ids)
    wide = jax.ShapeDtypeStruct((BLOCK, WIDE), bf16)
    narrow = jax.ShapeDtypeStruct((BLOCK, HEAD_DIM), bf16)
    return pl.pallas_call(
        write_out,
        out_shape=(wide, wide, narrow, narrow),
        in_specs=[pl.BlockSpec(memory_space=pltpu.VMEM)] * 3,
        out_specs=(any_space,) * 4,
        scratch_shapes=[dma((HEADS,)), dma((HEADS,)), dma((2,))],
        compiler_params=pltpu.CompilerParams(vmem_limit_bytes=1 << 20),
    )(*[pltpu.with_memory_space_constraint(out, pltpu.VMEM) for out in (att, dq, dkv)])


def solution(mesh):
    rows = P(("pb", "kv"), None)
    return jax.shard_map(
        local, mesh=mesh, in_specs=(rows, rows, rows, rows, P()),
        out_specs=(rows, rows, rows, rows), check_vma=False)
```

```python
import jax
import jax.numpy as jnp
from jax import lax
from jax.experimental import pallas as pl
from jax.experimental.pallas import tpu as pltpu
from jax.sharding import PartitionSpec as P

HEADS = 8
HEAD_DIM = 128
BLOCK = 128
NBLK = 256
WIDE = HEADS * HEAD_DIM

NEG = -1e30
SCALE = HEAD_DIM ** (-0.5)
LOG2E = 1.4426950408889634
EXP_SCALE = SCALE * LOG2E

MESH = pl.DeviceIdType.MESH
SEND_ORDER = (1, 2, 3, 4, 5, 6, 7)


def dot_nn(a, b):
    return lax.dot_general(a, b, (((1,), (0,)), ((), ())), preferred_element_type=jnp.float32)


def dot_nt(a, b):
    return lax.dot_general(a, b, (((1,), (1,)), ((), ())), preferred_element_type=jnp.float32)


def side_by_side(ref):
    return jnp.concatenate([ref[h] for h in range(HEADS)], axis=1)


def head_cols(h):
    return slice(h * HEAD_DIM, (h + 1) * HEAD_DIM)


def kernel(
    q_hbm, k_hbm, v_hbm, g_hbm, docs_hbm,
    att_out, dq_out, dkv_out,
    kv, q_in, g_in, qt, gt, probs, maxes, run_max, run_sum, out_acc, dq_acc, delta,
    w_a, ds_a, w_b, ds_b, ds_all, pg, r1r, r2s, r2r, r3s, r3b, r3r, one_back, r4b, r4r, total, docs,
    local_sem, q_sem, g_sem, docs_sem,
    kv_send, kv_recv, p_send, p_recv,
    r1_send, r1_recv, r2_send, r2_recv, r3_send, r3_recv, r4_send, r4_recv,
):
    pb = lax.axis_index("pb")
    kvi = lax.axis_index("kv")
    p = pb * 16 + kvi
    c = lax.rem(kvi, 2)
    y = lax.rem(lax.div(kvi, 2), 4)

    def seq_dev(delta_p):
        t = lax.rem(p + delta_p + NBLK, NBLK)
        return (lax.div(t, 16), lax.rem(t, 16))

    partner = (pb, kvi + 1 - 2 * c)
    chip = lax.div(p, 2)
    column = lax.div(p, 8)

    def there(e):
        return (chip + e >= 0) & (chip + e < NBLK // 2)

    @pl.when(column < 2)
    def _():
        for e in range(1, 9):
            kv[e, c] = jnp.zeros((2, BLOCK, HEAD_DIM), jnp.bfloat16)

    barrier = pltpu.get_barrier_semaphore()
    peers = [e for d in range(1, 9) for e in (d, -d)]
    count = jnp.int32(1)
    pl.semaphore_signal(barrier, inc=1, device_id=partner, device_id_type=MESH)
    for e in peers:
        count = count + there(e).astype(jnp.int32)

        @pl.when(there(e))
        def _():
            pl.semaphore_signal(barrier, inc=1, device_id=seq_dev(2 * e), device_id_type=MESH)

    own_k = pltpu.make_async_copy(k_hbm, kv.at[0, c, 0], local_sem.at[0])
    own_v = pltpu.make_async_copy(v_hbm, kv.at[0, c, 1], local_sem.at[1])
    own_k.start()
    own_v.start()
    docs_copy = pltpu.make_async_copy(docs_hbm, docs, docs_sem)
    docs_copy.start()
    q_copies = [
        pltpu.make_async_copy(q_hbm.at[:, head_cols(h)], q_in.at[h], q_sem.at[h]) for h in range(HEADS)]
    g_copies = [
        pltpu.make_async_copy(g_hbm.at[:, head_cols(h)], g_in.at[h], g_sem.at[h]) for h in range(HEADS)]
    for copy in q_copies + g_copies:
        copy.start()
    own_k.wait()
    own_v.wait()
    pl.semaphore_wait(barrier, count)

    def remote(src, dst, send_sem, recv_sem, dev):
        return pltpu.make_async_remote_copy(
            src_ref=src, dst_ref=dst, send_sem=send_sem, recv_sem=recv_sem,
            device_id=dev, device_id_type=MESH)

    def straight(e):
        return y + e < 8

    def kv_copy(e, passed):
        src = kv.at[8 if passed else 0, c]
        return remote(src, kv.at[e, c], kv_send.at[e], kv_recv.at[e], seq_dev(2 * e - (16 if passed else 0)))

    def kv_wait(e):
        @pl.when(there(-e))
        def _():
            remote(kv.at[0, c], kv.at[e, c], kv_send.at[e], kv_recv.at[e], partner).wait_recv()

    def p_copy(e):
        return remote(kv.at[e, c], kv.at[e, c], p_send.at[e], p_recv.at[e], partner)

    def special_copy():
        return remote(kv.at[8 * c, c], kv.at[0, c], p_send.at[0], p_recv.at[0], partner)

    two_on = there(8) & ((y > 0) | (c == 1))
    two_back = there(-8) & ((y > 0) | (c == 1))

    def two_wait():
        @pl.when(two_back)
        def _():
            remote(kv.at[0, c], kv.at[8, c], kv_send.at[8], kv_recv.at[8], partner).wait_recv()

    @pl.when(two_on & (y > 0))
    def _():
        kv_copy(8, False).start()

    for e in SEND_ORDER:
        @pl.when(straight(e) & there(e))
        def _():
            kv_copy(e, False).start()

    @pl.when(two_on & (y == 0))
    def _():
        kv_copy(8, False).start()

    @pl.when(c == 0)
    def _():
        special_copy().start()

    for h in range(HEADS):
        q_copies[h].wait()
        qt[h] = q_in[h].T
    docs_copy.wait()
    my_doc = docs[p]

    def bias_of(idx):
        same = (docs[jnp.maximum(idx, 0)] == my_doc) & (idx >= 0)
        return jnp.where(same, 0.0, NEG).astype(jnp.float32)

    def forward(keys, values_t, slot, parts, first):
        for h in range(HEADS):
            cols = head_cols(h)
            s = dot_nn(keys, qt[h])
            if first:
                key_at = lax.broadcasted_iota(jnp.int32, s.shape, 0)
                query_at = lax.broadcasted_iota(jnp.int32, s.shape, 1)
                s = jnp.where(key_at <= query_at, s, NEG)
            tops = []
            for lo, _, _, bias in parts:
                top = jnp.max(s[lo:lo + BLOCK], axis=0, keepdims=True) * EXP_SCALE
                tops.append(top if bias is None else top + bias)
            new_max = tops[0]
            for top in tops[1:]:
                new_max = jnp.maximum(new_max, top)
            if not first:
                old_max = run_max[:, cols]
                new_max = jnp.maximum(new_max, old_max)
                alpha = jnp.exp2(old_max - new_max)
            run_max[:, cols] = new_max
            total = None
            pieces = []
            for lo, at, parity, bias in parts:
                shift = -new_max if bias is None else bias - new_max
                piece = jnp.exp2(s[lo:lo + BLOCK] * EXP_SCALE + shift)
                part_sum = jnp.sum(piece, axis=0, keepdims=True)
                total = part_sum if total is None else total + part_sum
                piece = piece.astype(jnp.bfloat16)
                probs[slot, h, pl.ds(at, BLOCK)] = piece
                pieces.append(piece)
                maxes[slot, parity, :, cols] = new_max
            tile = pieces[0] if len(pieces) == 1 else jnp.concatenate(pieces, axis=0)
            mixed = dot_nn(values_t, tile)
            if first:
                run_sum[:, cols] = total
                out_acc[:, cols] = mixed
            else:
                run_sum[:, cols] = run_sum[:, cols] * alpha + total
                out_acc[:, cols] = out_acc[:, cols] * alpha + mixed

    c_rows = pl.multiple_of(c * BLOCK, BLOCK)
    o_rows = pl.multiple_of((1 - c) * BLOCK, BLOCK)
    forward(kv[0, c, 0], kv[0, c, 1].T, 0, [(0, c_rows, c, None)], True)

    @pl.when(y > 0)
    def _():
        two_wait()

        @pl.when(c == 1)
        def _():
            special_copy().start()

    for e in range(5, 8):
        @pl.when((y + e >= 8) & (column >= 2))
        def _():
            kv_copy(e, True).start()

    for e in (1, 2):
        kv_wait(e)
        p_copy(e).start()
    for h in range(HEADS):
        g_copies[h].wait()
        gt[h] = g_in[h].T

    def forward_step(e, carry):
        @pl.when(e < 6)
        def _():
            kv_wait(e + 2)
            p_copy(e + 2).start()

        @pl.when((e == 5) & (y == 0))
        def _():
            two_wait()

            @pl.when(c == 1)
            def _():
                special_copy().start()

        remote(kv.at[e, c], kv.at[e, 1 - c], p_send.at[e], p_recv.at[e], partner).wait_recv()
        keys = kv[e, :, 0].reshape(2 * BLOCK, HEAD_DIM)
        values_t = kv[e, :, 1].reshape(2 * BLOCK, HEAD_DIM).T
        base = p - c - 2 * e
        forward(keys, values_t, e, [(0, 0, 0, bias_of(base)), (BLOCK, BLOCK, 1, bias_of(base + 1))], False)
        return carry

    lax.fori_loop(1, 8, forward_step, 0)

    special_copy().wait_recv()
    special_at = jnp.where(c == 0, p - 15, p - 1)
    forward(kv[0, 1 - c, 0], kv[0, 1 - c, 1].T, 0, [(0, o_rows, 1 - c, bias_of(special_at))], False)

    for h in range(HEADS):
        cols = head_cols(h)
        inv = 1.0 / run_sum[:, cols]
        att_t = (out_acc[:, cols] * inv).astype(jnp.bfloat16)
        att_out[h] = att_t.T
        delta[:, cols] = jnp.sum(
            att_t.astype(jnp.float32) * gt[h].astype(jnp.float32), axis=0, keepdims=True)
        run_sum[:, cols] = inv

    def weigh(e, w_scr, ds_scr):
        values = kv[e, :, 1].reshape(2 * BLOCK, HEAD_DIM)
        for h in range(HEADS):
            cols = head_cols(h)
            gp = dot_nn(values, gt[h]) - delta[:, cols]
            for parity in (0, 1):
                rows = slice(parity * BLOCK, (parity + 1) * BLOCK)
                factor = jnp.exp2(maxes[e, parity, :, cols] - run_max[:, cols]) * run_sum[:, cols]
                w = probs[e, h, rows].astype(jnp.float32) * factor
                w_scr[h, rows] = w.astype(jnp.bfloat16)
                ds = (w * gp[rows]).astype(jnp.bfloat16)
                ds_scr[h, rows] = ds
                ds_all[e, h, rows] = ds

    def products(e, w_scr, ds_scr):
        dk_t = dot_nt(side_by_side(qt), side_by_side(ds_scr))
        dv_t = dot_nt(side_by_side(gt), side_by_side(w_scr))
        for parity in (0, 1):
            rows = slice(parity * BLOCK, (parity + 1) * BLOCK)
            pg[e, parity, 0] = dk_t[:, rows].astype(jnp.bfloat16)
            pg[e, parity, 1] = dv_t[:, rows].astype(jnp.bfloat16)

    def r1_copy(e):
        return remote(pg.at[e, 1 - c], r1r.at[e], r1_send.at[e], r1_recv.at[e], partner)

    def r3_copy():
        return remote(r3b, r3r, r3_send, r3_recv, seq_dev(-16))

    def beside(e):
        return (e == 3) & (y < 3) | (e == 5) & (y > 0) | (e == 7) & (y == 3) | (e == 1) & (y == 0)

    def r2_copy(e):
        passed = jnp.where(beside(e), 8, jnp.where(e > y + 4, 16, 0))
        return remote(r2s.at[e], r2r.at[e], r2_send.at[e], r2_recv.at[e], seq_dev(passed - 2 * e))

    def chip_sum(e):
        r1_copy(e).wait_recv()
        return pg[e, c].astype(jnp.float32) + r1r[e].astype(jnp.float32)

    def r4_copy():
        return remote(r4b, r4r, r4_send, r4_recv, seq_dev(-8))

    def pass_on(e):
        @pl.when(e != 4)
        def _():
            r2s[e] = chip_sum(e).astype(jnp.bfloat16)

            @pl.when(there(-e))
            def _():
                r2_copy(e).start()

    orders = [(0, 2, 3, 1, 7, 6, 5, 4), (0, 2, 3, 5, 7, 6, 4, 1), (0, 6, 3, 5, 7, 4, 2, 1), (0, 6, 5, 7, 4, 2, 3, 1)]
    codes = [sum(e << (3 * j) for j, e in enumerate(order)) for order in orders]
    turns = jnp.where(y == 0, codes[0], jnp.where(y == 1, codes[1], jnp.where(y == 2, codes[2], codes[3])))

    def turn(j):
        return lax.rem(lax.shift_right_logical(turns, 3 * jnp.asarray(j, jnp.int32)), 8)

    later_sum = y > 0
    beside_in = {1: y == 3, 3: y > 0, 5: y < 3, 7: y == 0}
    straight_in = {
        e: (y + e < 4) | there(e) & ((e == 6) & (y < 2) | (e == 2) & (y > 1)) for e in (1, 2, 3, 6)}
    r3_sent = there(-8) & ((y > 0) | (c == 1))
    r3_due = there(8) & ((y > 0) | (c == 1))

    def hand_over(j):
        r1_copy(turn(j)).start()

        @pl.when(j > 2)
        def _():
            pass_on(turn(j - 2))

        @pl.when((j == 2) & ~later_sum)
        def _():
            r1_copy(0).wait_recv()
            special = r1r[0].astype(jnp.float32)
            total[...] = pg[0, c].astype(jnp.float32) + jnp.where(c == 0, special, 0.0)

            @pl.when(there(-8) & (c == 1))
            def _():
                r3b[...] = r1r[0]
                r3_copy().start()

    weigh(turn(0), w_a, ds_a)

    def backward_steps(i, carry):
        j = 2 * i
        weigh(turn(j + 1), w_b, ds_b)
        products(turn(j), w_a, ds_a)
        hand_over(j)
        weigh(turn(j + 2), w_a, ds_a)
        products(turn(j + 1), w_b, ds_b)
        hand_over(j + 1)
        return carry

    lax.fori_loop(0, 3, backward_steps, 0)
    weigh(turn(7), w_b, ds_b)
    products(turn(6), w_a, ds_a)
    hand_over(jnp.int32(6))
    products(turn(7), w_b, ds_b)
    hand_over(jnp.int32(7))
    pass_on(turn(6))
    pass_on(turn(7))

    one_back[...] = chip_sum(4)
    for e in (1, 3, 5, 7):
        @pl.when(beside_in[e] & (column >= 1))
        def _():
            r2_copy(e).wait_recv()
            one_back[...] += r2r[e].astype(jnp.float32)

    @pl.when(there(-4))
    def _():
        r4b[...] = one_back[...].astype(jnp.bfloat16)
        r4_copy().start()

    @pl.when(later_sum)
    def _():
        r1_copy(0).wait_recv()
        special = r1r[0].astype(jnp.float32)
        total[...] = pg[0, c].astype(jnp.float32) + jnp.where(c == 0, special, 0.0)
        r3s[...] = jnp.where(c == 0, 0.0, special)

    for e in range(5, 8):
        @pl.when((y + e >= 8) & (column >= 2))
        def _():
            r2_copy(e).wait_recv()
            r3s[...] += r2r[e].astype(jnp.float32)

    @pl.when(there(-8) & (y > 0))
    def _():
        r3b[...] = r3s[...].astype(jnp.bfloat16)
        r3_copy().start()

    def query_grads(e, carry):
        keys_t = kv[e, :, 0].reshape(2 * BLOCK, HEAD_DIM).T
        dq_acc[...] += dot_nn(keys_t, side_by_side(ds_all.at[e]))
        return carry

    dq_acc[...] = dot_nn(kv[0, :, 0].reshape(2 * BLOCK, HEAD_DIM).T, side_by_side(ds_all.at[0]))
    lax.fori_loop(1, 8, query_grads, 0)
    for h in range(HEADS):
        dq_out[h] = (dq_acc[:, head_cols(h)] * SCALE).astype(jnp.bfloat16).T

    for e in (6, 3, 2, 1):
        @pl.when(straight_in[e])
        def _():
            r2_copy(e).wait_recv()
            total[...] += r2r[e].astype(jnp.float32)

    special_copy().wait_send()
    @pl.when(two_on)
    def _():
        kv_copy(8, False).wait_send()

    for e in range(1, 8):
        p_copy(e).wait_send()

        @pl.when(straight(e) & there(e) | (y + e >= 8) & (column >= 2))
        def _():
            kv_copy(e, False).wait_send()

        if e != 4:
            @pl.when(there(-e))
            def _():
                r2_copy(e).wait_send()

    for e in range(8):
        r1_copy(e).wait_send()


    @pl.when(there(4))
    def _():
        r4_copy().wait_recv()
        total[...] += r4r[...].astype(jnp.float32)

    @pl.when(r3_due)
    def _():
        r3_copy().wait_recv()
        total[...] += r3r[...].astype(jnp.float32)

    dkv_out[0] = (total[0] * SCALE).T.astype(jnp.bfloat16)
    dkv_out[1] = total[1].T.astype(jnp.bfloat16)

    @pl.when(r3_sent)
    def _():
        r3_copy().wait_send()

    @pl.when(there(-4))
    def _():
        r4_copy().wait_send()


def write_out(att, dq, dkv, att_hbm, dq_hbm, dk_hbm, dv_hbm, att_sem, dq_sem, dkv_sem):
    copies = []
    for h in range(HEADS):
        copies.append(pltpu.make_async_copy(att.at[h], att_hbm.at[:, head_cols(h)], att_sem.at[h]))
        copies.append(pltpu.make_async_copy(dq.at[h], dq_hbm.at[:, head_cols(h)], dq_sem.at[h]))
    copies.append(pltpu.make_async_copy(dkv.at[0], dk_hbm, dkv_sem.at[0]))
    copies.append(pltpu.make_async_copy(dkv.at[1], dv_hbm, dkv_sem.at[1]))
    for copy in copies:
        copy.start()
    for copy in copies:
        copy.wait()


def local(queries, key_rows, value_rows, out_grad, doc_ids):
    bf16, f32 = jnp.bfloat16, jnp.float32
    dma = pltpu.SemaphoreType.DMA
    any_space = pl.BlockSpec(memory_space=pl.ANY)
    pair = (2, BLOCK, HEAD_DIM)
    by_head = (HEADS, BLOCK, HEAD_DIM)
    att, dq, dkv = pl.pallas_call(
        kernel,
        out_shape=(pltpu.VMEM(by_head, bf16), pltpu.VMEM(by_head, bf16), pltpu.VMEM(pair, bf16)),
        in_specs=[any_space] * 5,
        out_specs=(pl.BlockSpec(memory_space=pltpu.VMEM),) * 3,
        scratch_shapes=[
            pltpu.VMEM((9, 2) + pair, bf16),
            pltpu.VMEM((HEADS, BLOCK, HEAD_DIM), bf16),
            pltpu.VMEM((HEADS, BLOCK, HEAD_DIM), bf16),
            pltpu.VMEM((HEADS, HEAD_DIM, BLOCK), bf16),
            pltpu.VMEM((HEADS, HEAD_DIM, BLOCK), bf16),
            pltpu.VMEM((8, HEADS, 2 * BLOCK, BLOCK), bf16),
            pltpu.VMEM((8, 2, 1, WIDE), f32),
            pltpu.VMEM((1, WIDE), f32),
            pltpu.VMEM((1, WIDE), f32),
            pltpu.VMEM((HEAD_DIM, WIDE), f32),
            pltpu.VMEM((HEAD_DIM, WIDE), f32),
            pltpu.VMEM((1, WIDE), f32),
            pltpu.VMEM((HEADS, 2 * BLOCK, BLOCK), bf16),
            pltpu.VMEM((HEADS, 2 * BLOCK, BLOCK), bf16),
            pltpu.VMEM((HEADS, 2 * BLOCK, BLOCK), bf16),
            pltpu.VMEM((HEADS, 2 * BLOCK, BLOCK), bf16),
            pltpu.VMEM((8, HEADS, 2 * BLOCK, BLOCK), bf16),
            pltpu.VMEM((8, 2) + pair, bf16),
            pltpu.VMEM((8,) + pair, bf16),
            pltpu.VMEM((8,) + pair, bf16),
            pltpu.VMEM((8,) + pair, bf16),
            pltpu.VMEM(pair, f32),
            pltpu.VMEM(pair, bf16),
            pltpu.VMEM(pair, bf16),
            pltpu.VMEM(pair, f32),
            pltpu.VMEM(pair, bf16),
            pltpu.VMEM(pair, bf16),
            pltpu.VMEM(pair, f32),
            pltpu.SMEM((NBLK,), jnp.int32),
            dma((2,)), dma((HEADS,)), dma((HEADS,)),
            dma,
            dma((9,)), dma((9,)), dma((8,)), dma((8,)),
            dma((8,)), dma((8,)), dma((8,)), dma((8,)), dma, dma, dma, dma,
        ],
        compiler_params=pltpu.CompilerParams(collective_id=0, has_side_effects=True),
    )(queries, key_rows, value_rows, out_grad, doc_ids)
    wide = jax.ShapeDtypeStruct((BLOCK, WIDE), bf16)
    narrow = jax.ShapeDtypeStruct((BLOCK, HEAD_DIM), bf16)
    return pl.pallas_call(
        write_out,
        out_shape=(wide, wide, narrow, narrow),
        in_specs=[pl.BlockSpec(memory_space=pltpu.VMEM)] * 3,
        out_specs=(any_space,) * 4,
        scratch_shapes=[dma((HEADS,)), dma((HEADS,)), dma((2,))],
        compiler_params=pltpu.CompilerParams(vmem_limit_bytes=1 << 20),
    )(*[pltpu.with_memory_space_constraint(out, pltpu.VMEM) for out in (att, dq, dkv)])


def solution(mesh):
    rows = P(("pb", "kv"), None)
    return jax.shard_map(
        local, mesh=mesh, in_specs=(rows, rows, rows, rows, P()),
        out_specs=(rows, rows, rows, rows), check_vma=False)
```

```python
import jax
import jax.numpy as jnp
from jax import lax
from jax.experimental import pallas as pl
from jax.experimental.pallas import tpu as pltpu
from jax.sharding import PartitionSpec as P

HEADS = 8
HEAD_DIM = 128
BLOCK = 128
NBLK = 256
WIDE = HEADS * HEAD_DIM

NEG = -1e30
SCALE = HEAD_DIM ** (-0.5)
LOG2E = 1.4426950408889634
EXP_SCALE = SCALE * LOG2E

MESH = pl.DeviceIdType.MESH
SEND_ORDER = (1, 2, 3, 4, 5, 6, 7)


def dot_nn(a, b):
    return lax.dot_general(a, b, (((1,), (0,)), ((), ())), preferred_element_type=jnp.float32)


def dot_nt(a, b):
    return lax.dot_general(a, b, (((1,), (1,)), ((), ())), preferred_element_type=jnp.float32)


def side_by_side(ref):
    return jnp.concatenate([ref[h] for h in range(HEADS)], axis=1)


def head_cols(h):
    return slice(h * HEAD_DIM, (h + 1) * HEAD_DIM)


def kernel(
    q_hbm, k_hbm, v_hbm, g_hbm, docs_hbm,
    att_out, dq_out, dkv_out,
    kv, q_in, g_in, qt, gt, probs, maxes, run_max, run_sum, out_acc, dq_acc, delta,
    w_a, ds_a, w_b, ds_b, ds_all, att_ts, pg, r1r, r2s, r2r, r3s, r3b, r3r, one_back, r4b, r4r, total, docs,
    local_sem, q_sem, g_sem, docs_sem,
    kv_send, kv_recv, p_send, p_recv,
    r1_send, r1_recv, r2_send, r2_recv, r3_send, r3_recv, r4_send, r4_recv,
):
    pb = lax.axis_index("pb")
    kvi = lax.axis_index("kv")
    p = pb * 16 + kvi
    c = lax.rem(kvi, 2)
    y = lax.rem(lax.div(kvi, 2), 4)

    def seq_dev(delta_p):
        t = lax.rem(p + delta_p + NBLK, NBLK)
        return (lax.div(t, 16), lax.rem(t, 16))

    partner = (pb, kvi + 1 - 2 * c)
    chip = lax.div(p, 2)
    column = lax.div(p, 8)

    def there(e):
        return (chip + e >= 0) & (chip + e < NBLK // 2)

    @pl.when(column < 2)
    def _():
        for e in range(1, 9):
            kv[e, c] = jnp.zeros((2, BLOCK, HEAD_DIM), jnp.bfloat16)

    barrier = pltpu.get_barrier_semaphore()
    peers = [e for d in range(8, 0, -1) for e in (d, -d)]
    count = jnp.int32(1)
    pl.semaphore_signal(barrier, inc=1, device_id=partner, device_id_type=MESH)
    for e in peers:
        count = count + there(e).astype(jnp.int32)

        @pl.when(there(e))
        def _():
            pl.semaphore_signal(barrier, inc=1, device_id=seq_dev(2 * e), device_id_type=MESH)

    own_k = pltpu.make_async_copy(k_hbm, kv.at[0, c, 0], local_sem.at[0])
    own_v = pltpu.make_async_copy(v_hbm, kv.at[0, c, 1], local_sem.at[1])
    own_k.start()
    own_v.start()
    docs_copy = pltpu.make_async_copy(docs_hbm, docs, docs_sem)
    docs_copy.start()
    q_copies = [
        pltpu.make_async_copy(q_hbm.at[:, head_cols(h)], q_in.at[h], q_sem.at[h]) for h in range(HEADS)]
    g_copies = [
        pltpu.make_async_copy(g_hbm.at[:, head_cols(h)], g_in.at[h], g_sem.at[h]) for h in range(HEADS)]
    for copy in q_copies + g_copies:
        copy.start()
    own_k.wait()
    own_v.wait()
    pl.semaphore_wait(barrier, count)

    def remote(src, dst, send_sem, recv_sem, dev):
        return pltpu.make_async_remote_copy(
            src_ref=src, dst_ref=dst, send_sem=send_sem, recv_sem=recv_sem,
            device_id=dev, device_id_type=MESH)

    def straight(e):
        return y + e < 8

    def kv_copy(e, passed):
        src = kv.at[8 if passed else 0, c]
        return remote(src, kv.at[e, c], kv_send.at[e], kv_recv.at[e], seq_dev(2 * e - (16 if passed else 0)))

    def kv_wait(e):
        @pl.when(there(-e))
        def _():
            remote(kv.at[0, c], kv.at[e, c], kv_send.at[e], kv_recv.at[e], partner).wait_recv()

    def p_copy(e):
        return remote(kv.at[e, c], kv.at[e, c], p_send.at[e], p_recv.at[e], partner)

    def special_copy():
        return remote(kv.at[8 * c, c], kv.at[0, c], p_send.at[0], p_recv.at[0], partner)

    two_on = there(8) & ((y > 0) | (c == 1))
    two_back = there(-8) & ((y > 0) | (c == 1))

    def two_wait():
        @pl.when(two_back)
        def _():
            remote(kv.at[0, c], kv.at[8, c], kv_send.at[8], kv_recv.at[8], partner).wait_recv()

    @pl.when(two_on & (y > 0))
    def _():
        kv_copy(8, False).start()

    for e in SEND_ORDER:
        @pl.when(straight(e) & there(e))
        def _():
            kv_copy(e, False).start()

    @pl.when(two_on & (y == 0))
    def _():
        kv_copy(8, False).start()

    @pl.when(c == 0)
    def _():
        special_copy().start()

    for h in range(HEADS):
        q_copies[h].wait()
        qt[h] = q_in[h].T
    docs_copy.wait()
    my_doc = docs[p]

    def bias_of(idx):
        same = (docs[jnp.maximum(idx, 0)] == my_doc) & (idx >= 0)
        return jnp.where(same, 0.0, NEG).astype(jnp.float32)

    def forward(keys, values_t, slot, parts, first):
        for h in range(HEADS):
            cols = head_cols(h)
            s = dot_nn(keys, qt[h])
            if first:
                key_at = lax.broadcasted_iota(jnp.int32, s.shape, 0)
                query_at = lax.broadcasted_iota(jnp.int32, s.shape, 1)
                s = jnp.where(key_at <= query_at, s, NEG)
            tops = []
            for lo, _, _, bias in parts:
                top = jnp.max(s[lo:lo + BLOCK], axis=0, keepdims=True) * EXP_SCALE
                tops.append(top if bias is None else top + bias)
            new_max = tops[0]
            for top in tops[1:]:
                new_max = jnp.maximum(new_max, top)
            if not first:
                old_max = run_max[:, cols]
                new_max = jnp.maximum(new_max, old_max)
                alpha = jnp.exp2(old_max - new_max)
            run_max[:, cols] = new_max
            total = None
            pieces = []
            for lo, at, parity, bias in parts:
                shift = -new_max if bias is None else bias - new_max
                piece = jnp.exp2(s[lo:lo + BLOCK] * EXP_SCALE + shift)
                part_sum = jnp.sum(piece, axis=0, keepdims=True)
                total = part_sum if total is None else total + part_sum
                piece = piece.astype(jnp.bfloat16)
                probs[slot, h, pl.ds(at, BLOCK)] = piece
                pieces.append(piece)
                maxes[slot, parity, :, cols] = new_max
            tile = pieces[0] if len(pieces) == 1 else jnp.concatenate(pieces, axis=0)
            mixed = dot_nn(values_t, tile)
            if first:
                run_sum[:, cols] = total
                out_acc[:, cols] = mixed
            else:
                run_sum[:, cols] = run_sum[:, cols] * alpha + total
                out_acc[:, cols] = out_acc[:, cols] * alpha + mixed

    c_rows = pl.multiple_of(c * BLOCK, BLOCK)
    o_rows = pl.multiple_of((1 - c) * BLOCK, BLOCK)
    forward(kv[0, c, 0], kv[0, c, 1].T, 0, [(0, c_rows, c, None)], True)

    @pl.when(y > 0)
    def _():
        two_wait()

        @pl.when(c == 1)
        def _():
            special_copy().start()

    for e in range(5, 8):
        @pl.when((y + e >= 8) & (column >= 2))
        def _():
            kv_copy(e, True).start()

    for e in (1, 2):
        kv_wait(e)
        p_copy(e).start()
    for h in range(HEADS):
        g_copies[h].wait()
        gt[h] = g_in[h].T

    def forward_step(e, carry):
        @pl.when(e < 6)
        def _():
            kv_wait(e + 2)
            p_copy(e + 2).start()

        @pl.when((e == 5) & (y == 0))
        def _():
            two_wait()

            @pl.when(c == 1)
            def _():
                special_copy().start()

        remote(kv.at[e, c], kv.at[e, 1 - c], p_send.at[e], p_recv.at[e], partner).wait_recv()
        keys = kv[e, :, 0].reshape(2 * BLOCK, HEAD_DIM)
        values_t = kv[e, :, 1].reshape(2 * BLOCK, HEAD_DIM).T
        base = p - c - 2 * e
        forward(keys, values_t, e, [(0, 0, 0, bias_of(base)), (BLOCK, BLOCK, 1, bias_of(base + 1))], False)
        return carry

    lax.fori_loop(1, 8, forward_step, 0)

    special_copy().wait_recv()
    special_at = jnp.where(c == 0, p - 15, p - 1)
    forward(kv[0, 1 - c, 0], kv[0, 1 - c, 1].T, 0, [(0, o_rows, 1 - c, bias_of(special_at))], False)

    for h in range(HEADS):
        cols = head_cols(h)
        inv = 1.0 / run_sum[:, cols]
        att_t = (out_acc[:, cols] * inv).astype(jnp.bfloat16)
        att_ts[h] = att_t
        delta[:, cols] = jnp.sum(
            att_t.astype(jnp.float32) * gt[h].astype(jnp.float32), axis=0, keepdims=True)
        run_sum[:, cols] = inv

    def weigh(e, w_scr, ds_scr):
        values = kv[e, :, 1].reshape(2 * BLOCK, HEAD_DIM)
        for h in range(HEADS):
            cols = head_cols(h)
            gp = dot_nn(values, gt[h]) - delta[:, cols]
            for parity in (0, 1):
                rows = slice(parity * BLOCK, (parity + 1) * BLOCK)
                factor = jnp.exp2(maxes[e, parity, :, cols] - run_max[:, cols]) * run_sum[:, cols]
                w = probs[e, h, rows].astype(jnp.float32) * factor
                w_scr[h, rows] = w.astype(jnp.bfloat16)
                ds = (w * gp[rows]).astype(jnp.bfloat16)
                ds_scr[h, rows] = ds
                ds_all[e, h, rows] = ds

    def products(e, w_scr, ds_scr):
        dk_t = dot_nt(side_by_side(qt), side_by_side(ds_scr))
        dv_t = dot_nt(side_by_side(gt), side_by_side(w_scr))
        for parity in (0, 1):
            rows = slice(parity * BLOCK, (parity + 1) * BLOCK)
            pg[e, parity, 0] = dk_t[:, rows].astype(jnp.bfloat16)
            pg[e, parity, 1] = dv_t[:, rows].astype(jnp.bfloat16)

    def r1_copy(e):
        return remote(pg.at[e, 1 - c], r1r.at[e], r1_send.at[e], r1_recv.at[e], partner)

    def r3_copy():
        return remote(r3b, r3r, r3_send, r3_recv, seq_dev(-16))

    def beside(e):
        return (e == 3) & (y < 3) | (e == 5) & (y > 0) | (e == 7) & (y == 3) | (e == 1) & (y == 0)

    def r2_copy(e):
        passed = jnp.where(beside(e), 8, jnp.where(e > y + 4, 16, 0))
        return remote(r2s.at[e], r2r.at[e], r2_send.at[e], r2_recv.at[e], seq_dev(passed - 2 * e))

    def chip_sum(e):
        r1_copy(e).wait_recv()
        return pg[e, c].astype(jnp.float32) + r1r[e].astype(jnp.float32)

    def r4_copy():
        return remote(r4b, r4r, r4_send, r4_recv, seq_dev(-8))

    def pass_on(e):
        @pl.when(e != 4)
        def _():
            r2s[e] = chip_sum(e).astype(jnp.bfloat16)

            @pl.when(there(-e))
            def _():
                r2_copy(e).start()

    orders = [(0, 2, 3, 1, 7, 6, 5, 4), (0, 2, 3, 5, 7, 6, 4, 1), (0, 6, 3, 5, 7, 4, 2, 1), (0, 6, 5, 7, 4, 2, 3, 1)]
    codes = [sum(e << (3 * j) for j, e in enumerate(order)) for order in orders]
    turns = jnp.where(y == 0, codes[0], jnp.where(y == 1, codes[1], jnp.where(y == 2, codes[2], codes[3])))

    def turn(j):
        return lax.rem(lax.shift_right_logical(turns, 3 * jnp.asarray(j, jnp.int32)), 8)

    later_sum = y > 0
    beside_in = {1: y == 3, 3: y > 0, 5: y < 3, 7: y == 0}
    straight_in = {
        e: (y + e < 4) | there(e) & ((e == 6) & (y < 2) | (e == 2) & (y > 1)) for e in (1, 2, 3, 6)}
    r3_sent = there(-8) & ((y > 0) | (c == 1))
    r3_due = there(8) & ((y > 0) | (c == 1))

    def hand_over(j):
        r1_copy(turn(j)).start()

        @pl.when(j > 2)
        def _():
            pass_on(turn(j - 2))

        @pl.when((j == 2) & ~later_sum)
        def _():
            r1_copy(0).wait_recv()
            special = r1r[0].astype(jnp.float32)
            total[...] = pg[0, c].astype(jnp.float32) + jnp.where(c == 0, special, 0.0)

            @pl.when(there(-8) & (c == 1))
            def _():
                r3b[...] = r1r[0]
                r3_copy().start()

    weigh(turn(0), w_a, ds_a)

    def backward_steps(i, carry):
        j = 2 * i
        weigh(turn(j + 1), w_b, ds_b)
        products(turn(j), w_a, ds_a)
        hand_over(j)
        weigh(turn(j + 2), w_a, ds_a)
        products(turn(j + 1), w_b, ds_b)
        hand_over(j + 1)
        return carry

    lax.fori_loop(0, 3, backward_steps, 0)
    weigh(turn(7), w_b, ds_b)
    products(turn(6), w_a, ds_a)
    hand_over(jnp.int32(6))
    products(turn(7), w_b, ds_b)
    hand_over(jnp.int32(7))
    pass_on(turn(6))
    pass_on(turn(7))

    one_back[...] = chip_sum(4)
    for e in (1, 3, 5, 7):
        @pl.when(beside_in[e] & (column >= 1))
        def _():
            r2_copy(e).wait_recv()
            one_back[...] += r2r[e].astype(jnp.float32)

    @pl.when(there(-4))
    def _():
        r4b[...] = one_back[...].astype(jnp.bfloat16)
        r4_copy().start()

    @pl.when(later_sum)
    def _():
        r1_copy(0).wait_recv()
        special = r1r[0].astype(jnp.float32)
        total[...] = pg[0, c].astype(jnp.float32) + jnp.where(c == 0, special, 0.0)
        r3s[...] = jnp.where(c == 0, 0.0, special)

    for e in range(5, 8):
        @pl.when((y + e >= 8) & (column >= 2))
        def _():
            r2_copy(e).wait_recv()
            r3s[...] += r2r[e].astype(jnp.float32)

    @pl.when(there(-8) & (y > 0))
    def _():
        r3b[...] = r3s[...].astype(jnp.bfloat16)
        r3_copy().start()

    def query_grads(e, carry):
        keys_t = kv[e, :, 0].reshape(2 * BLOCK, HEAD_DIM).T
        dq_acc[...] += dot_nn(keys_t, side_by_side(ds_all.at[e]))
        return carry

    dq_acc[...] = dot_nn(kv[0, :, 0].reshape(2 * BLOCK, HEAD_DIM).T, side_by_side(ds_all.at[0]))
    lax.fori_loop(1, 8, query_grads, 0)
    for h in range(HEADS):
        att_out[h] = att_ts[h].T
        dq_out[h] = (dq_acc[:, head_cols(h)] * SCALE).astype(jnp.bfloat16).T

    for e in (6, 3, 2, 1):
        @pl.when(straight_in[e])
        def _():
            r2_copy(e).wait_recv()
            total[...] += r2r[e].astype(jnp.float32)

    special_copy().wait_send()
    @pl.when(two_on)
    def _():
        kv_copy(8, False).wait_send()

    for e in range(1, 8):
        p_copy(e).wait_send()

        @pl.when(straight(e) & there(e) | (y + e >= 8) & (column >= 2))
        def _():
            kv_copy(e, False).wait_send()

        if e != 4:
            @pl.when(there(-e))
            def _():
                r2_copy(e).wait_send()

    for e in range(8):
        r1_copy(e).wait_send()


    @pl.when(there(4))
    def _():
        r4_copy().wait_recv()
        total[...] += r4r[...].astype(jnp.float32)

    @pl.when(r3_due)
    def _():
        r3_copy().wait_recv()
        total[...] += r3r[...].astype(jnp.float32)

    dkv_out[0] = (total[0] * SCALE).T.astype(jnp.bfloat16)
    dkv_out[1] = total[1].T.astype(jnp.bfloat16)

    @pl.when(r3_sent)
    def _():
        r3_copy().wait_send()

    @pl.when(there(-4))
    def _():
        r4_copy().wait_send()


def write_out(att, dq, dkv, att_hbm, dq_hbm, dk_hbm, dv_hbm, att_sem, dq_sem, dkv_sem):
    copies = []
    for h in range(HEADS):
        copies.append(pltpu.make_async_copy(att.at[h], att_hbm.at[:, head_cols(h)], att_sem.at[h]))
        copies.append(pltpu.make_async_copy(dq.at[h], dq_hbm.at[:, head_cols(h)], dq_sem.at[h]))
    copies.append(pltpu.make_async_copy(dkv.at[0], dk_hbm, dkv_sem.at[0]))
    copies.append(pltpu.make_async_copy(dkv.at[1], dv_hbm, dkv_sem.at[1]))
    for copy in copies:
        copy.start()
    for copy in copies:
        copy.wait()


def local(queries, key_rows, value_rows, out_grad, doc_ids):
    bf16, f32 = jnp.bfloat16, jnp.float32
    dma = pltpu.SemaphoreType.DMA
    any_space = pl.BlockSpec(memory_space=pl.ANY)
    pair = (2, BLOCK, HEAD_DIM)
    by_head = (HEADS, BLOCK, HEAD_DIM)
    att, dq, dkv = pl.pallas_call(
        kernel,
        out_shape=(pltpu.VMEM(by_head, bf16), pltpu.VMEM(by_head, bf16), pltpu.VMEM(pair, bf16)),
        in_specs=[any_space] * 5,
        out_specs=(pl.BlockSpec(memory_space=pltpu.VMEM),) * 3,
        scratch_shapes=[
            pltpu.VMEM((9, 2) + pair, bf16),
            pltpu.VMEM((HEADS, BLOCK, HEAD_DIM), bf16),
            pltpu.VMEM((HEADS, BLOCK, HEAD_DIM), bf16),
            pltpu.VMEM((HEADS, HEAD_DIM, BLOCK), bf16),
            pltpu.VMEM((HEADS, HEAD_DIM, BLOCK), bf16),
            pltpu.VMEM((8, HEADS, 2 * BLOCK, BLOCK), bf16),
            pltpu.VMEM((8, 2, 1, WIDE), f32),
            pltpu.VMEM((1, WIDE), f32),
            pltpu.VMEM((1, WIDE), f32),
            pltpu.VMEM((HEAD_DIM, WIDE), f32),
            pltpu.VMEM((HEAD_DIM, WIDE), f32),
            pltpu.VMEM((1, WIDE), f32),
            pltpu.VMEM((HEADS, 2 * BLOCK, BLOCK), bf16),
            pltpu.VMEM((HEADS, 2 * BLOCK, BLOCK), bf16),
            pltpu.VMEM((HEADS, 2 * BLOCK, BLOCK), bf16),
            pltpu.VMEM((HEADS, 2 * BLOCK, BLOCK), bf16),
            pltpu.VMEM((8, HEADS, 2 * BLOCK, BLOCK), bf16),
            pltpu.VMEM((HEADS, HEAD_DIM, BLOCK), bf16),
            pltpu.VMEM((8, 2) + pair, bf16),
            pltpu.VMEM((8,) + pair, bf16),
            pltpu.VMEM((8,) + pair, bf16),
            pltpu.VMEM((8,) + pair, bf16),
            pltpu.VMEM(pair, f32),
            pltpu.VMEM(pair, bf16),
            pltpu.VMEM(pair, bf16),
            pltpu.VMEM(pair, f32),
            pltpu.VMEM(pair, bf16),
            pltpu.VMEM(pair, bf16),
            pltpu.VMEM(pair, f32),
            pltpu.SMEM((NBLK,), jnp.int32),
            dma((2,)), dma((HEADS,)), dma((HEADS,)),
            dma,
            dma((9,)), dma((9,)), dma((8,)), dma((8,)),
            dma((8,)), dma((8,)), dma((8,)), dma((8,)), dma, dma, dma, dma,
        ],
        compiler_params=pltpu.CompilerParams(collective_id=0, has_side_effects=True),
    )(queries, key_rows, value_rows, out_grad, doc_ids)
    wide = jax.ShapeDtypeStruct((BLOCK, WIDE), bf16)
    narrow = jax.ShapeDtypeStruct((BLOCK, HEAD_DIM), bf16)
    return pl.pallas_call(
        write_out,
        out_shape=(wide, wide, narrow, narrow),
        in_specs=[pl.BlockSpec(memory_space=pltpu.VMEM)] * 3,
        out_specs=(any_space,) * 4,
        scratch_shapes=[dma((HEADS,)), dma((HEADS,)), dma((2,))],
        compiler_params=pltpu.CompilerParams(vmem_limit_bytes=1 << 20),
    )(*[pltpu.with_memory_space_constraint(out, pltpu.VMEM) for out in (att, dq, dkv)])


def solution(mesh):
    rows = P(("pb", "kv"), None)
    return jax.shard_map(
        local, mesh=mesh, in_specs=(rows, rows, rows, rows, P()),
        out_specs=(rows, rows, rows, rows), check_vma=False)
```
